32 devices in a mesh: ep: 16 (over z, x, core), tp: 2 (over y).
Axes of the slice: x: 2, y: 2, z: 4, core: 2. Of those that a mesh axis runs over, the one named last changes fastest.
Arguments:
- tokens: bfloat16 [4096, 1024], P('ep'), may hold values from -6 to 6
- sequence_number: int32 [4096], P('ep'), may hold values from 0 to 15, as said below
- expert_routes: int32 [2, 4096, 8], P(None, 'ep'), may hold values from 0 to 15, all different within a row; in each aligned block of 256 rows (0 to 255, 256 to 511, ..., all dimensions but the last counted through in order) at most 192 rows name the same one
- attention_gain: float32 [2, 1024], replicated, may hold values from 0.5 to 1.5
- query_weight: bfloat16 [2, 1024, 1024], P(None, None, 'tp')
- key_matrix: bfloat16 [2, 1024, 512], P(None, None, 'tp')
- value_matrix: bfloat16 [2, 1024, 512], P(None, None, 'tp'), may hold values from -0.1875 to 0.1875
- output_weight: bfloat16 [2, 1024, 1024], P(None, 'tp'), may hold values from -0.75 to 0.75
- mixer_gain: float32 [2, 1024], replicated, may hold values from 0.5 to 1.5
- router_weight: bfloat16 [2, 1024, 16], replicated
- gate_weight: bfloat16 [2, 16, 1024, 512], P(None, 'ep', None, 'tp'), may hold values from -0.1875 to 0.1875
- up_weight: bfloat16 [2, 16, 1024, 512], P(None, 'ep', None, 'tp'), may hold values from -0.1875 to 0.1875
- down_weight: bfloat16 [2, 16, 512, 1024], P(None, 'ep', 'tp'), may hold values from -1.5 to 1.5
- output_grad: float32 [4096, 1024], P('ep'), may hold values from -6 to 6
Outputs:
- block_output: bfloat16 [4096, 1024], P('ep')
- input_grad: float32 [4096, 1024], P('ep')
- grad_attention_gain: float32 [2, 1024], replicated
- grad_query_weight: float32 [2, 1024, 1024], P(None, None, 'tp')
- grad_key_weight: float32 [2, 1024, 512], P(None, None, 'tp')
- grad_value_weight: float32 [2, 1024, 512], P(None, None, 'tp')
- grad_output_weight: float32 [2, 1024, 1024], P(None, 'tp')
- grad_mixer_gain: float32 [2, 1024], replicated
- grad_router_weight: float32 [2, 1024, 16], replicated
- grad_gate_weight: float32 [2, 16, 1024, 512], P(None, 'ep', None, 'tp')
- grad_up_weight: float32 [2, 16, 1024, 512], P(None, 'ep', None, 'tp')
- grad_down_weight: float32 [2, 16, 512, 1024], P(None, 'ep', 'tp')
The draws below stay inside these ranges and needn't reach their ends.
Inputs may be any that keep to these rules, and one draw needn't show every extreme that they name: `sequence_number`: within each aligned block of 256 rows the numbers start at 0 and rise by 0 or 1 from a row to the next; a block holds at most max(2, 16) sequences, and some block holds exactly that many; in at least one block all 256 rows form one sequence. `expert_routes`: each token names 8 different experts in each layer. In each layer the 256 rows of one device name any one expert at most 192 times, a bound that some block reaches.
All inputs are finite; a program needn't handle non-finite values.
Results may differ from the reference program's by a relative error of at most 0.038.
Values may be sent and summed in bfloat16 or wider, within the bound.
No kernel may reach another device: no remote copies, remote signals or barrier semaphores. Data moves between devices by JAX's collectives and lax.ppermute only.
A program may use at most 256 MiB of HBM per device.

```python
import math
import jax
import jax.numpy as jnp
import numpy as np
from jax import lax

MODEL_DIMENSION = 1024
QUERY_HEADS = 16
KEY_VALUE_HEADS = 8
HEAD_DIMENSION = 64
FF = 512
TOPK = 8
DECODER_LAYERS = 2
TOKENS_PER_RANK = 256
EXPERTS = 16
TOKEN_TOTAL = 4096
CAP = 192
N_EP = 16


def scaled_heads(key, rows_in, heads, head_size):
    base_key = jax.random.fold_in(key, 0)
    base = jax.random.normal(base_key, (DECODER_LAYERS, rows_in, heads, head_size), jnp.float32) * rows_in ** (-0.5)
    return base.reshape(DECODER_LAYERS, rows_in, heads * head_size).astype(jnp.bfloat16)


def draw_query_weight(key, part):
    return scaled_heads(jax.random.fold_in(key, 17), MODEL_DIMENSION, QUERY_HEADS, HEAD_DIMENSION)


def draw_key_matrix(key, part):
    return scaled_heads(jax.random.fold_in(key, 29), MODEL_DIMENSION, KEY_VALUE_HEADS, HEAD_DIMENSION)


def draw_router_weight(key, part):
    base_key = jax.random.fold_in(jax.random.fold_in(key, 41), 0)
    base = jax.random.normal(base_key, (DECODER_LAYERS, MODEL_DIMENSION, EXPERTS), jnp.float32) * (0.35 * MODEL_DIMENSION ** (-0.5))
    return base.astype(jnp.bfloat16)


def draw_sequence_number(key, part):
    count_key, order_key, whole_key = jax.random.split(jax.random.fold_in(key, 53), 3)
    most_count = max(2, TOKENS_PER_RANK // 16)
    counts = jax.random.randint(count_key, (N_EP,), 1, most_count + 1)
    whole_row = jax.random.randint(whole_key, (), 0, N_EP)
    fullest_row = (whole_row + 1) % N_EP
    row_numbers = jnp.arange(N_EP, dtype=jnp.int32)
    counts = jnp.where(row_numbers == whole_row, 1, counts)
    counts = jnp.where(row_numbers == fullest_row, most_count, counts)
    row_keys = jax.random.split(order_key, N_EP)
    orders = jax.vmap(lambda row_key: jax.random.permutation(row_key, TOKENS_PER_RANK - 1) + 1)(row_keys).astype(jnp.int32)
    keep = jnp.arange(TOKENS_PER_RANK - 1, dtype=jnp.int32)[None, :] < counts[:, None] - 1
    starts_here = jnp.zeros((N_EP, TOKENS_PER_RANK), jnp.int32).at[row_numbers[:, None], orders].set(keep.astype(jnp.int32))
    numbers = jnp.cumsum(starts_here, axis=1)
    return numbers.reshape(-1).astype(jnp.int32)


def shard_levels(key, extent, pieces, low, high):
    loudness, own = 1.0, jax.random.fold_in(key, 6)
    for axis_at, parts in pieces:
        draws = jnp.exp(jax.random.uniform(jax.random.fold_in(own, axis_at), (parts,), jnp.float32, low / len(pieces), high / len(pieces)))
        loudness = loudness * jnp.repeat(draws, extent[axis_at] // parts).reshape([-1 if axis == axis_at else 1 for axis in range(len(extent))])
    return loudness


def shared_out(key, own, number, rows, number_of, top, most, lean):
    order = jax.random.permutation(key, number_of)
    packed, common = portions_of(number_of, rows * top, most, lean, True), portions_of(number_of, rows * top, most, lean, False)
    places = jnp.arange(number_of)

    def named(sizes, turn):
        used = int((sizes > 0).sum())
        fixed = max(1, used // 4)
        passed = fixed + (places - fixed + turn * (used - fixed)) % max(1, number_of - fixed)
        return jnp.zeros((number_of,), jnp.int32).at[order[jnp.where(places < fixed, places, passed)]].set(jnp.asarray(sizes, jnp.int32))

    sizes = jnp.where(number % 4 == 0, named(packed, number // 4), named(common, number - number // 4 - 1))
    mixed = jax.random.permutation(jax.random.fold_in(own, 3), number_of)
    donor, receiver = mixed[0:number_of // 2 * 2:2], mixed[1:number_of // 2 * 2:2]
    margin = jnp.minimum(sizes[donor] - 1, most - sizes[receiver]) // 2
    margin = jnp.where((donor == order[0]) | (receiver == order[0]) | (sizes[receiver] == 0), 0, jnp.maximum(margin, 0))
    passed = jax.random.randint(jax.random.fold_in(own, 4), (number_of // 2,), 0, 1 << 20) % (margin + 1)
    sizes = sizes.at[donor].add(-passed).at[receiver].add(passed)
    labels = jnp.searchsorted(jnp.cumsum(sizes), jnp.arange(rows * top), side="right").astype(jnp.int32)
    table = labels.reshape(top, rows).T
    table = table[jax.random.permutation(jax.random.fold_in(own, 1), rows)]
    turn = jax.random.randint(jax.random.fold_in(own, 2), (rows, 1), 0, top)
    return jnp.take_along_axis(table, (jnp.arange(top)[None, :] + turn) % top, axis=1)


def portions_of(number_of, total, reach, slope, full):
    loads = [(1 << 20) // math.isqrt(rank ** slope) + 1 for rank in range(1, number_of + 1)]
    largest = reach if full else min(reach, max(-(-total // number_of), total * loads[0] // sum(loads)))
    least = 1 if total - largest >= number_of - 1 else 0
    holding, surplus = [largest] + [least] * (number_of - 1), total - largest - least * (number_of - 1)
    while surplus > 0:
        candidates = [i for i in range(1, number_of) if holding[i] < largest] or [i for i in range(1, number_of) if holding[i] < reach]
        pool, left = sum([loads[i] for i in candidates]), surplus
        for i in candidates:
            extra = min(reach - holding[i], max(1, left * loads[i] // pool), surplus)
            holding[i] = holding[i] + extra
            surplus = surplus - extra
    return np.array(holding)


def bell_draw(rng, shape, width, reach, shards=(), held_as=jnp.bfloat16):
    values = jax.random.normal(rng, shape, jnp.float32) * width
    if len(shards) > 0:
        values = shard_levels(rng, shape, shards, -0.22, 0.18) * values
    return jnp.clip(values, min=-reach, max=reach).astype(held_as)


def setup_inputs(seed: int = 0) -> dict:
    key_of = jax.random.split(jax.random.key(seed), 15)
    tokens = bell_draw(key_of[0], (TOKEN_TOTAL, MODEL_DIMENSION), 1.0, 6.0, ((0, 16),))
    sequence_number = draw_sequence_number(jax.random.fold_in(key_of[14], 71), 0)
    expert_routes_keys = jax.random.split(jax.random.fold_in(key_of[2], 1), DECODER_LAYERS * TOKEN_TOTAL // TOKENS_PER_RANK)
    expert_routes_turns = jax.random.permutation(jax.random.fold_in(key_of[2], 3), DECODER_LAYERS * TOKEN_TOTAL // TOKENS_PER_RANK)
    expert_routes = jax.vmap(lambda own, number: shared_out(jax.random.fold_in(key_of[2], 2), own, number, TOKENS_PER_RANK, EXPERTS, TOPK, CAP, 4))(expert_routes_keys, expert_routes_turns).reshape((DECODER_LAYERS, TOKEN_TOTAL, TOPK))
    attention_gain = jnp.clip(1.0 + 0.1 * jax.random.normal(key_of[3], (DECODER_LAYERS, MODEL_DIMENSION), jnp.float32), 0.5, 1.5)
    query_weight = draw_query_weight(jax.random.fold_in(key_of[14], 71), 0)
    key_matrix = draw_key_matrix(jax.random.fold_in(key_of[14], 71), 0)
    value_matrix = bell_draw(key_of[6], (DECODER_LAYERS, MODEL_DIMENSION, KEY_VALUE_HEADS * HEAD_DIMENSION), MODEL_DIMENSION ** -0.5, 0.1875, ((2, 2),))
    output_weight = bell_draw(key_of[7], (DECODER_LAYERS, QUERY_HEADS * HEAD_DIMENSION, MODEL_DIMENSION), (QUERY_HEADS * HEAD_DIMENSION // 16) ** -0.5, 0.75, ((1, 2),))
    mixer_gain = jnp.clip(1.0 + 0.1 * jax.random.normal(key_of[8], (DECODER_LAYERS, MODEL_DIMENSION), jnp.float32), 0.5, 1.5)
    router_weight = draw_router_weight(jax.random.fold_in(key_of[14], 71), 0)
    gate_weight = bell_draw(key_of[10], (DECODER_LAYERS, EXPERTS, MODEL_DIMENSION, FF), MODEL_DIMENSION ** -0.5, 0.1875, ((1, 16), (3, 2)))
    up_weight = bell_draw(key_of[11], (DECODER_LAYERS, EXPERTS, MODEL_DIMENSION, FF), MODEL_DIMENSION ** -0.5, 0.1875, ((1, 16), (3, 2)))
    down_weight = bell_draw(key_of[12], (DECODER_LAYERS, EXPERTS, FF, MODEL_DIMENSION), (FF // 32) ** -0.5, 1.5, ((1, 16), (2, 2)))
    output_grad = bell_draw(key_of[13], (TOKEN_TOTAL, MODEL_DIMENSION), 1.0, 6.0, ((0, 16),), jnp.float32)
    return {"tokens": tokens, "sequence_number": sequence_number, "expert_routes": expert_routes, "attention_gain": attention_gain, "query_weight": query_weight, "key_matrix": key_matrix, "value_matrix": value_matrix, "output_weight": output_weight, "mixer_gain": mixer_gain, "router_weight": router_weight, "gate_weight": gate_weight, "up_weight": up_weight, "down_weight": down_weight, "output_grad": output_grad}


EPS = 1e-06
THETA = 10000.0
SCALE = 0.125
NEGATIVE = -1e+30

def positions(sequence_row):
    index_row = jnp.arange(sequence_row.shape[0], dtype=jnp.int32)
    numbers = sequence_row.astype(jnp.int32)
    previous = jnp.concatenate([jnp.full((1,), -1, jnp.int32), numbers[:-1]])
    starts_at = jnp.where(numbers != previous, index_row, 0).astype(jnp.int32)
    return (index_row - lax.cummax(starts_at, axis=0)).astype(jnp.float32)

def rope_tables(position_row, head_size):
    half_size = head_size // 2
    frequency = THETA ** (-(jnp.arange(half_size, dtype=jnp.float32) * 2.0 / head_size))
    angle_table = position_row[:, None] * frequency[None, :]
    return (jnp.cos(angle_table)[:, None, :], jnp.sin(angle_table)[:, None, :])

def apply_rotary(values, cosine_table, sine_table):
    half_size = values.shape[-1] // 2
    first_half = values[..., :half_size]
    second_half = values[..., half_size:]
    return jnp.concatenate([first_half * cosine_table - second_half * sine_table, second_half * cosine_table + first_half * sine_table], axis=-1)

def reverse_rotary(values, cosine_table, sine_table):
    half_size = values.shape[-1] // 2
    first_half = values[..., :half_size]
    second_half = values[..., half_size:]
    return jnp.concatenate([first_half * cosine_table + second_half * sine_table, second_half * cosine_table - first_half * sine_table], axis=-1)

def rms_forward(stream, gain):
    inverse_rms = lax.rsqrt(lax.optimization_barrier(jnp.mean(stream * stream, axis=-1, keepdims=True)) + EPS)
    normal_part = stream * inverse_rms
    return (normal_part, inverse_rms, (normal_part * gain).astype(jnp.bfloat16))

def rms_backward(normed_grad, normal_part, inverse_rms, gain):
    scaled_grad = normed_grad * gain
    stream_grad = inverse_rms * (scaled_grad - normal_part * lax.optimization_barrier(jnp.mean(scaled_grad * normal_part, axis=-1, keepdims=True)))
    return (stream_grad, lax.optimization_barrier(jnp.sum(normed_grad * normal_part, axis=0)))

def head_scores(query_block, projected_keys, sequence_block, index_block, sequence_row, index_row):
    scores = jnp.einsum('qngd,knd->ngqk', query_block.astype(jnp.float32), projected_keys.astype(jnp.float32)) * SCALE
    allowed = (sequence_block[:, None] == sequence_row[None, :]) & (index_row[None, :] <= index_block[:, None])
    return (jnp.where(allowed, scores, NEGATIVE), allowed)

def attend(projected_queries, projected_keys, projected_values, sequence_row):
    total_rows = projected_queries.shape[0]
    row_block = min(512, total_rows)
    index_row = jnp.arange(total_rows, dtype=jnp.int32)

    def one_block(block_start):
        query_block = lax.dynamic_slice_in_dim(projected_queries, block_start, row_block, 0)
        sequence_block = lax.dynamic_slice_in_dim(sequence_row, block_start, row_block, 0)
        index_block = lax.dynamic_slice_in_dim(index_row, block_start, row_block, 0)
        scores, allowed = head_scores(query_block, projected_keys, sequence_block, index_block, sequence_row, index_row)
        row_max = lax.optimization_barrier(jnp.max(scores, axis=-1, keepdims=True))
        exp_scores = jnp.exp(scores - row_max)
        row_total = lax.optimization_barrier(jnp.sum(exp_scores, axis=-1, keepdims=True))
        attention_probs = (exp_scores / row_total).astype(jnp.bfloat16)
        block_out = jnp.einsum('ngqk,knd->qngd', attention_probs.astype(jnp.float32), projected_values.astype(jnp.float32)).astype(jnp.bfloat16)
        return (block_out, (row_max + jnp.log(row_total))[..., 0])
    block_starts = jnp.arange(total_rows // row_block, dtype=jnp.int32) * row_block
    block_outs, log_total = lax.map(one_block, block_starts)
    return (block_outs.reshape(projected_queries.shape), log_total)

def attend_back(projected_queries, projected_keys, projected_values, sequence_row, log_total, mixed_grad):
    total_rows = projected_queries.shape[0]
    row_block = min(512, total_rows)
    index_row = jnp.arange(total_rows, dtype=jnp.int32)

    def one_block(carried, block_item):
        block_start, block_log = block_item
        query_block = lax.dynamic_slice_in_dim(projected_queries, block_start, row_block, 0)
        sequence_block = lax.dynamic_slice_in_dim(sequence_row, block_start, row_block, 0)
        index_block = lax.dynamic_slice_in_dim(index_row, block_start, row_block, 0)
        grad_block = lax.dynamic_slice_in_dim(mixed_grad, block_start, row_block, 0)
        scores, allowed = head_scores(query_block, projected_keys, sequence_block, index_block, sequence_row, index_row)
        prob_exact = jnp.where(allowed, jnp.exp(scores - block_log[..., None]), 0.0)
        prob_grad = jnp.einsum('qngd,knd->ngqk', grad_block.astype(jnp.float32), projected_values.astype(jnp.float32))
        row_dot = lax.optimization_barrier(jnp.sum(prob_exact * prob_grad, axis=-1, keepdims=True))
        score_grad = (prob_exact * (prob_grad - row_dot) * SCALE).astype(jnp.bfloat16).astype(jnp.float32)
        probs_half = prob_exact.astype(jnp.bfloat16).astype(jnp.float32)
        key_gradient, value_gradient = carried
        value_gradient = value_gradient + jnp.einsum('ngqk,qngd->knd', probs_half, grad_block.astype(jnp.float32))
        key_gradient = key_gradient + jnp.einsum('ngqk,qngd->knd', score_grad, query_block.astype(jnp.float32))
        query_grad = jnp.einsum('ngqk,knd->qngd', score_grad, projected_keys.astype(jnp.float32))
        return ((key_gradient, value_gradient), query_grad)
    block_starts = jnp.arange(total_rows // row_block, dtype=jnp.int32) * row_block
    zero_keys = jnp.zeros(projected_keys.shape, jnp.float32)
    (key_gradient, value_gradient), query_grad = lax.scan(one_block, (zero_keys, zero_keys), (block_starts, log_total))
    return (query_grad.reshape(projected_queries.shape), key_gradient, value_gradient)

def slot_tables(route_ids):
    blocks = route_ids.reshape(N_EP, TOKENS_PER_RANK * TOPK).astype(jnp.int32)
    hit_table = (blocks[:, :, None] == jnp.arange(EXPERTS, dtype=jnp.int32)[None, None, :]).astype(jnp.int32)
    running = jnp.cumsum(hit_table, axis=1).astype(jnp.int32)
    slot_index = (lax.optimization_barrier(jnp.sum(running * hit_table, axis=-1)) - 1).astype(jnp.int32)
    flat_index = jnp.arange(TOKENS_PER_RANK * TOPK, dtype=jnp.int32)
    source = jnp.arange(N_EP, dtype=jnp.int32)[:, None]
    token_rows = (source * TOKENS_PER_RANK + flat_index[None, :] // TOPK).astype(jnp.int32).reshape(-1)
    route_rank = jnp.broadcast_to(flat_index[None, :] % TOPK, blocks.shape).astype(jnp.int32).reshape(-1)
    slot_place = (blocks * (N_EP * CAP) + source * CAP + slot_index).astype(jnp.int32).reshape(-1)
    size_all = EXPERTS * N_EP * CAP
    token_of = jnp.zeros((size_all,), jnp.int32).at[slot_place].set(token_rows)
    rank_of = jnp.zeros((size_all,), jnp.int32).at[slot_place].set(route_rank)
    slot_live = jnp.zeros((size_all,), jnp.float32).at[slot_place].set(1.0)
    return (token_of.reshape(EXPERTS, N_EP * CAP), rank_of.reshape(EXPERTS, N_EP * CAP), slot_live.reshape(EXPERTS, N_EP * CAP))

def reference(tokens, sequence_number, expert_routes, attention_gain, query_weight, key_matrix, value_matrix, output_weight, mixer_gain, router_weight, gate_weight, up_weight, down_weight, output_grad):
    query_group_size = QUERY_HEADS // KEY_VALUE_HEADS
    sequence_blocks = sequence_number.reshape(N_EP, TOKENS_PER_RANK).astype(jnp.int32)
    position_all = jax.vmap(positions)(sequence_blocks).reshape(-1)
    cosine_table, sine_table = rope_tables(position_all, HEAD_DIMENSION)
    stream = tokens.astype(jnp.float32)
    saved = []
    for current_layer in range(DECODER_LAYERS):
        normal_one, inverse_one, first_normalized = rms_forward(stream, attention_gain[current_layer])
        projected_queries = jnp.dot(first_normalized, query_weight[current_layer], preferred_element_type=jnp.float32).reshape(TOKEN_TOTAL, QUERY_HEADS, HEAD_DIMENSION)
        projected_queries = apply_rotary(projected_queries, cosine_table, sine_table).astype(jnp.bfloat16).reshape(N_EP, TOKENS_PER_RANK, KEY_VALUE_HEADS, query_group_size, HEAD_DIMENSION)
        projected_keys = jnp.dot(first_normalized, key_matrix[current_layer], preferred_element_type=jnp.float32).reshape(TOKEN_TOTAL, KEY_VALUE_HEADS, HEAD_DIMENSION)
        projected_keys = apply_rotary(projected_keys, cosine_table, sine_table).astype(jnp.bfloat16).reshape(N_EP, TOKENS_PER_RANK, KEY_VALUE_HEADS, HEAD_DIMENSION)
        projected_values = jnp.dot(first_normalized, value_matrix[current_layer], preferred_element_type=jnp.float32).astype(jnp.bfloat16).reshape(N_EP, TOKENS_PER_RANK, KEY_VALUE_HEADS, HEAD_DIMENSION)

        def attend_device(device_item):
            return attend(device_item[0], device_item[1], device_item[2], device_item[3])
        mixed_heads, log_total = lax.map(attend_device, (projected_queries, projected_keys, projected_values, sequence_blocks))
        mixed_flat = mixed_heads.reshape(TOKEN_TOTAL, QUERY_HEADS * HEAD_DIMENSION)
        residual = stream + jnp.dot(mixed_flat, output_weight[current_layer], preferred_element_type=jnp.float32)
        normal_two, inverse_two, normed_two = rms_forward(residual, mixer_gain[current_layer])
        route_ids = expert_routes[current_layer].astype(jnp.int32)
        logits = jnp.dot(normed_two, router_weight[current_layer], preferred_element_type=jnp.float32)
        route_table = (route_ids[:, :, None] == jnp.arange(EXPERTS, dtype=jnp.int32)[None, None, :]).astype(jnp.float32)
        gate_probs = jax.nn.softmax(lax.optimization_barrier(jnp.sum(route_table * logits[:, None, :], axis=-1)), axis=-1)
        token_of, rank_of, slot_live = slot_tables(route_ids)
        gate_layer = gate_weight[current_layer]
        up_layer = up_weight[current_layer]
        down_layer = down_weight[current_layer]

        def expert_step(mixture, expert_index):
            token_rows = token_of[expert_index]
            live_rows = slot_live[expert_index]
            inputs = jnp.where(live_rows[:, None] > 0, normed_two[token_rows], jnp.zeros((), jnp.bfloat16)).astype(jnp.bfloat16)
            gate_part = jnp.dot(inputs, gate_layer[expert_index], preferred_element_type=jnp.float32)
            up_part = jnp.dot(inputs, up_layer[expert_index], preferred_element_type=jnp.float32)
            hidden = (jax.nn.silu(gate_part) * up_part).astype(jnp.bfloat16)
            expert_out = jnp.dot(hidden, down_layer[expert_index], preferred_element_type=jnp.float32).astype(jnp.bfloat16)
            route_gate = gate_probs[token_rows, rank_of[expert_index]] * live_rows
            return (mixture.at[token_rows].add(route_gate[:, None] * expert_out.astype(jnp.float32)), None)
        mixture, ignored = lax.scan(expert_step, jnp.zeros((TOKEN_TOTAL, MODEL_DIMENSION), jnp.float32), jnp.arange(EXPERTS, dtype=jnp.int32))
        saved.append((normal_one, inverse_one, first_normalized, projected_queries, projected_keys, projected_values, mixed_flat, log_total, normal_two, inverse_two, normed_two, route_table, gate_probs, token_of, rank_of, slot_live))
        stream = residual + mixture
    block_output = stream.astype(jnp.bfloat16)
    stream_grad = output_grad.astype(jnp.float32)
    collected = [None] * DECODER_LAYERS
    for current_layer in reversed(range(DECODER_LAYERS)):
        normal_one, inverse_one, first_normalized, projected_queries, projected_keys, projected_values, mixed_flat, log_total, normal_two, inverse_two, normed_two, route_table, gate_probs, token_of, rank_of, slot_live = saved[current_layer]
        gate_layer = gate_weight[current_layer]
        up_layer = up_weight[current_layer]
        down_layer = down_weight[current_layer]
        outer_grad = stream_grad

        def expert_back(carried, expert_index):
            normed_grad, gate_grad = carried
            token_rows = token_of[expert_index]
            rank_rows = rank_of[expert_index]
            live_rows = slot_live[expert_index]
            inputs = jnp.where(live_rows[:, None] > 0, normed_two[token_rows], jnp.zeros((), jnp.bfloat16)).astype(jnp.bfloat16)
            gate_part = jnp.dot(inputs, gate_layer[expert_index], preferred_element_type=jnp.float32)
            up_part = jnp.dot(inputs, up_layer[expert_index], preferred_element_type=jnp.float32)
            activated = jax.nn.silu(gate_part)
            sigmoid_gate = jax.nn.sigmoid(gate_part)
            hidden = (activated * up_part).astype(jnp.bfloat16)
            expert_out = jnp.dot(hidden, down_layer[expert_index], preferred_element_type=jnp.float32).astype(jnp.bfloat16)
            out_rows = outer_grad[token_rows]
            gate_grad_rows = lax.optimization_barrier(jnp.sum(out_rows * expert_out.astype(jnp.float32), axis=-1)) * live_rows
            route_gate = gate_probs[token_rows, rank_rows] * live_rows
            out_grad = (route_gate[:, None] * out_rows).astype(jnp.bfloat16)
            hidden_grad = jnp.dot(out_grad, down_layer[expert_index].T, preferred_element_type=jnp.float32)
            act_grad = (hidden_grad * up_part * sigmoid_gate * (1.0 + gate_part * (1.0 - sigmoid_gate))).astype(jnp.bfloat16)
            up_grad = (hidden_grad * activated).astype(jnp.bfloat16)
            down_term = jnp.dot(hidden.T, out_grad, preferred_element_type=jnp.float32)
            gate_term = jnp.dot(inputs.T, act_grad, preferred_element_type=jnp.float32)
            up_term = jnp.dot(inputs.T, up_grad, preferred_element_type=jnp.float32)
            input_rows = (jnp.dot(act_grad, gate_layer[expert_index].T, preferred_element_type=jnp.float32) + jnp.dot(up_grad, up_layer[expert_index].T, preferred_element_type=jnp.float32)).astype(jnp.bfloat16)
            normed_grad = normed_grad.at[token_rows].add(input_rows.astype(jnp.float32) * live_rows[:, None])
            gate_grad = gate_grad.at[token_rows, rank_rows].add(gate_grad_rows)
            return ((normed_grad, gate_grad), (gate_term, up_term, down_term))
        start_carry = (jnp.zeros((TOKEN_TOTAL, MODEL_DIMENSION), jnp.float32), jnp.zeros((TOKEN_TOTAL, TOPK), jnp.float32))
        (normed_grad, gate_grad), (grad_gate, grad_up, grad_down) = lax.scan(expert_back, start_carry, jnp.arange(EXPERTS, dtype=jnp.int32))
        weighted = lax.optimization_barrier(jnp.sum(gate_probs * gate_grad, axis=-1, keepdims=True))
        select_grad = gate_probs * (gate_grad - weighted)
        logit_grad = lax.optimization_barrier(jnp.sum(route_table * select_grad[:, :, None], axis=1)).astype(jnp.bfloat16)
        grad_router = jnp.dot(normed_two.T, logit_grad, preferred_element_type=jnp.float32)
        normed_grad = normed_grad + jnp.dot(logit_grad, router_weight[current_layer].T, preferred_element_type=jnp.float32)
        residual_part, grad_mixer = rms_backward(normed_grad, normal_two, inverse_two, mixer_gain[current_layer])
        residual_grad = stream_grad + residual_part
        residual_half = residual_grad.astype(jnp.bfloat16)
        grad_output = jnp.dot(mixed_flat.T, residual_half, preferred_element_type=jnp.float32)
        mixed_grad = jnp.dot(residual_half, output_weight[current_layer].T, preferred_element_type=jnp.float32).astype(jnp.bfloat16).reshape(projected_queries.shape)

        def back_device(device_item):
            return attend_back(device_item[0], device_item[1], device_item[2], device_item[3], device_item[4], device_item[5])
        query_grad, key_gradient, value_gradient = lax.map(back_device, (projected_queries, projected_keys, projected_values, sequence_blocks, log_total, mixed_grad))
        query_back = reverse_rotary(query_grad.reshape(TOKEN_TOTAL, QUERY_HEADS, HEAD_DIMENSION), cosine_table, sine_table).astype(jnp.bfloat16).reshape(TOKEN_TOTAL, QUERY_HEADS * HEAD_DIMENSION)
        key_reverse = reverse_rotary(key_gradient.reshape(TOKEN_TOTAL, KEY_VALUE_HEADS, HEAD_DIMENSION), cosine_table, sine_table).astype(jnp.bfloat16).reshape(TOKEN_TOTAL, KEY_VALUE_HEADS * HEAD_DIMENSION)
        value_reverse = value_gradient.astype(jnp.bfloat16).reshape(TOKEN_TOTAL, KEY_VALUE_HEADS * HEAD_DIMENSION)
        grad_query = jnp.dot(first_normalized.T, query_back, preferred_element_type=jnp.float32)
        grad_key = jnp.dot(first_normalized.T, key_reverse, preferred_element_type=jnp.float32)
        grad_value = jnp.dot(first_normalized.T, value_reverse, preferred_element_type=jnp.float32)
        normed_one_grad = jnp.dot(query_back, query_weight[current_layer].T, preferred_element_type=jnp.float32) + jnp.dot(key_reverse, key_matrix[current_layer].T, preferred_element_type=jnp.float32) + jnp.dot(value_reverse, value_matrix[current_layer].T, preferred_element_type=jnp.float32)
        stream_part, grad_attention = rms_backward(normed_one_grad, normal_one, inverse_one, attention_gain[current_layer])
        stream_grad = residual_grad + stream_part
        collected[current_layer] = (grad_attention, grad_query, grad_key, grad_value, grad_output, grad_mixer, grad_router, grad_gate, grad_up, grad_down)
    stacked = [jnp.stack([layer_grads[number] for layer_grads in collected]) for number in range(10)]
    return (block_output, stream_grad, stacked[0], stacked[1], stacked[2], stacked[3], stacked[4], stacked[5], stacked[6], stacked[7], stacked[8], stacked[9])
```

```python
import jax
import jax.numpy as jnp
from jax import lax
from jax.sharding import PartitionSpec as P

HEAD = 64
EPS = 1e-06
THETA = 10000.0
SCALE = 0.125
NEGATIVE = -1e30
BF = jnp.bfloat16
F32 = jnp.float32


def mm(a, b):
    return jnp.dot(a, b, preferred_element_type=F32)


def mm_nt(a, b):
    return lax.dot_general(a, b, (((1,), (1,)), ((), ())), preferred_element_type=F32)


def mm_tn(a, b):
    return lax.dot_general(a, b, (((0,), (0,)), ((), ())), preferred_element_type=F32)


class Grid:
    def __init__(self, mesh):
        self.ep, self.tp = mesh.shape["ep"], mesh.shape["tp"]
        self.nc = 2 if self.ep % 2 == 0 else 1
        rest = self.ep // self.nc
        self.nz = 4 if rest % 4 == 0 else 1
        self.nx = rest // self.nz

    def move(self, value, dz=0, dx=0, dc=0, dt=0):
        pairs = []
        for z in range(self.nz):
            for x in range(self.nx):
                for c in range(self.nc):
                    for t in range(self.tp):
                        there = self.at(z + dz, x + dx, c + dc) * self.tp + (t + dt) % self.tp
                        pairs.append((self.at(z, x, c) * self.tp + t, there))
        return lax.ppermute(value, ("ep", "tp"), pairs)

    def at(self, z, x, c):
        return ((z % self.nz) * self.nx + x % self.nx) * self.nc + c % self.nc

    def slots(self):
        return [
            (k, j, d) for k in range(self.nz) for j in range(self.nx) for d in range(self.nc)
        ]

    def slot_owner(self, slot):
        me = lax.axis_index("ep")
        z, x, c = me // (self.nx * self.nc), (me // self.nc) % self.nx, me % self.nc
        z, x, c = (z - slot[0]) % self.nz, (x - slot[1]) % self.nx, (c - slot[2]) % self.nc
        return (z * self.nx + x) * self.nc + c

    def gather_ep(self, own):
        found = {(0, 0, 0): own}
        for k in range(self.nz):
            if k:
                found[k, 0, 0] = self.move(found[k - 1, 0, 0], dz=1)
            for j in range(1, self.nx):
                found[k, j, 0] = self.move(found[k, j - 1, 0], dx=1)
            for j in range(self.nx):
                for d in range(1, self.nc):
                    found[k, j, d] = self.move(found[k, j, d - 1], dc=1)
        return [found[slot] for slot in self.slots()]

    def scatter_ep(self, parts):
        part = dict(zip(self.slots(), parts, strict=True))
        terms = []
        for k in [*range(self.nz // 2, self.nz), *reversed(range(self.nz // 2))]:
            line = []
            for j in range(self.nx):
                total = part[k, j, self.nc - 1]
                for d in reversed(range(self.nc - 1)):
                    arrived = self.move(total, dc=1)
                    total = (arrived.astype(F32) + part[k, j, d].astype(F32)).astype(BF)
                line.append(total)
            total = line[-1]
            for j in reversed(range(self.nx - 1)):
                arrived = self.move(total, dx=-1)
                total = (arrived.astype(F32) + line[j].astype(F32)).astype(BF)
            terms.append(self.move(total, dz=-k) if k else total)
        return sum(term.astype(F32) for term in terms)

    def gather_tp(self, own):
        found = [own]
        for _ in range(1, self.tp):
            found.append(self.move(found[-1], dt=1))
        return found

    def scatter_tp(self, parts):
        total = parts[0]
        for i in range(1, self.tp):
            total = total + self.move(parts[i].astype(BF), dt=-i).astype(F32)
        return total


def tp_block(whole, i, tp, axis=0):
    rows = whole.shape[axis] // tp
    start = ((lax.axis_index("tp") - i) % tp) * rows
    return lax.dynamic_slice_in_dim(whole, start, rows, axis)


def tp_join(blocks):
    tp, rows = len(blocks), blocks[0].shape[0]
    whole = jnp.zeros((tp * rows,) + blocks[0].shape[1:], blocks[0].dtype)
    for i, block in enumerate(blocks):
        start = ((lax.axis_index("tp") - i) % tp) * rows
        whole = lax.dynamic_update_slice_in_dim(whole, block, start, 0)
    return whole


def rope_tables(sequence_row):
    index_row = jnp.arange(sequence_row.shape[0], dtype=jnp.int32)
    same = sequence_row[:, None] == sequence_row[None, :]
    position = jnp.sum((same & (index_row[None, :] < index_row[:, None])).astype(jnp.int32), axis=1)
    half = HEAD // 2
    frequency = THETA ** (-(jnp.arange(half, dtype=F32) * 2.0 / HEAD))
    angle = position.astype(F32)[:, None] * frequency[None, :]
    allowed = same & (index_row[None, :] <= index_row[:, None])
    return jnp.cos(angle)[:, None, :], jnp.sin(angle)[:, None, :], allowed


def rotate(values, cosine, sine):
    first, second = values[..., : HEAD // 2], values[..., HEAD // 2 :]
    return jnp.concatenate(
        [first * cosine - second * sine, second * cosine + first * sine], axis=-1
    )


def rms(stream, gain):
    inverse = lax.rsqrt(jnp.mean(stream * stream, axis=-1, keepdims=True) + EPS)
    unit = stream * inverse
    return unit, inverse, (unit * gain).astype(BF)


def rms_back(grad, unit, inverse, gain):
    scaled = grad * gain
    back = inverse * (scaled - unit * jnp.mean(scaled * unit, axis=-1, keepdims=True))
    return back, jnp.sum(grad * unit, axis=0)


def attend(x, w, tables):
    cosine, sine, allowed = tables
    rows = x.shape[0]
    heads, groups = w["q"].shape[1] // HEAD, w["k"].shape[1] // HEAD
    q = rotate(mm(x, w["q"]).reshape(rows, heads, HEAD), cosine, sine).astype(BF)
    q = q.reshape(rows, groups, heads // groups, HEAD)
    k = rotate(mm(x, w["k"]).reshape(rows, groups, HEAD), cosine, sine).astype(BF)
    v = mm(x, w["v"]).astype(BF).reshape(rows, groups, HEAD)
    score = jnp.einsum("qngd,knd->ngqk", q, k, preferred_element_type=F32) * SCALE
    score = jnp.where(allowed, score, NEGATIVE)
    raised = jnp.exp(score - jnp.max(score, axis=-1, keepdims=True))
    probs = raised / jnp.sum(raised, axis=-1, keepdims=True)
    mixed = jnp.einsum("ngqk,knd->qngd", probs.astype(BF), v, preferred_element_type=F32)
    mixed = mixed.astype(BF).reshape(rows, heads * HEAD)
    return mm(mixed, w["o"]), (q, k, v, probs, mixed)


def attend_back(half, x, w, tables, kept):
    cosine, sine, allowed = tables
    q, k, v, probs, mixed = kept
    rows = x.shape[0]
    grad_o = mm_tn(mixed, half)
    mixed_grad = mm_nt(half, w["o"]).astype(BF).reshape(q.shape)
    prob_grad = jnp.einsum("qngd,knd->ngqk", mixed_grad, v, preferred_element_type=F32)
    row_dot = jnp.sum(probs * prob_grad, axis=-1, keepdims=True)
    score_grad = (probs * (prob_grad - row_dot) * SCALE).astype(BF)
    dv = jnp.einsum("ngqk,qngd->knd", probs.astype(BF), mixed_grad, preferred_element_type=F32)
    dk = jnp.einsum("ngqk,qngd->knd", score_grad, q, preferred_element_type=F32)
    dq = jnp.einsum("ngqk,knd->qngd", score_grad, k, preferred_element_type=F32)
    dq = rotate(dq.reshape(rows, -1, HEAD), cosine, -sine).astype(BF).reshape(rows, -1)
    dk = rotate(dk, cosine, -sine).astype(BF).reshape(rows, -1)
    dv = dv.astype(BF).reshape(rows, -1)
    grad_in = mm_nt(dq, w["q"]) + mm_nt(dk, w["k"]) + mm_nt(dv, w["v"])
    return grad_in, (mm_tn(x, dq), mm_tn(x, dk), mm_tn(x, dv), grad_o)


def gates(normed, router, chosen):
    logits = jnp.where(chosen, mm(normed, router), NEGATIVE)
    raised = jnp.where(chosen, jnp.exp(logits - jnp.max(logits, axis=-1, keepdims=True)), 0.0)
    return raised / jnp.sum(raised, axis=-1, keepdims=True)


def expert(x, chosen, w):
    gate_all = gates(x, w["router"], chosen)
    p = lax.dynamic_slice_in_dim(gate_all, lax.axis_index("ep"), 1, 1)
    a, u = mm(x, w["gate"]), mm(x, w["up"])
    h = jax.nn.silu(a) * u
    scaled = (p * h).astype(BF)
    return mm(scaled, w["down"]).astype(BF), (p, a, u, h, scaled)


def expert_back(x, sg, w, kept):
    p, a, u, h, scaled = kept
    raw = mm_nt(sg, w["down"])
    pg = p * jnp.sum(h * raw, axis=-1, keepdims=True)
    hidden_grad = p * raw
    s = jax.nn.sigmoid(a)
    da = (hidden_grad * u * s * (1.0 + a * (1.0 - s))).astype(BF)
    du = (hidden_grad * (a * s)).astype(BF)
    here = lax.dynamic_slice_in_dim(w["router"], lax.axis_index("ep"), 1, 1)
    back = mm_nt(da, w["gate"]) + mm_nt(du, w["up"]) + pg * here.astype(F32).reshape(1, -1)
    column = jnp.sum(x.astype(F32) * pg, axis=0)
    mine = jnp.arange(w["router"].shape[1]) == lax.axis_index("ep")
    grad_router = jnp.where(mine[:, None], column[None, :], 0.0)
    return back.astype(BF), (mm_tn(x, da), mm_tn(x, du), mm_tn(scaled, sg), grad_router)


def split(whole, count):
    rows = whole.shape[0] // count
    return [whole[i * rows : (i + 1) * rows] for i in range(count)]


def on_device(grid, tokens, sequence_number, routes, a_gain, qw, kw, vw, ow, m_gain, router, gw, uw, dw, output_grad):
    tp, ep = grid.tp, grid.ep
    layers, experts = qw.shape[0], router.shape[2]
    assert gw.shape[1] == 1 and experts == ep
    slots = len(grid.slots())
    tables = rope_tables(sequence_number)

    own_routes = tp_block(routes, 0, tp, 1)
    chosen = jnp.any(
        own_routes[..., None] == jnp.arange(experts, dtype=jnp.int32), axis=2
    ).astype(BF)
    every = lax.all_gather(chosen, "ep", axis=0)
    owners = jnp.stack([grid.slot_owner(slot) for slot in grid.slots()])
    every = every[owners].transpose(1, 0, 2, 3).reshape(layers, -1, experts) > 0
    chosen = chosen > 0

    weights = []
    for layer in range(layers):
        weights.append({
            "q": qw[layer], "k": kw[layer], "v": vw[layer], "o": ow[layer],
            "router": router[layer],
            "gate": jnp.concatenate(grid.gather_tp(gw[layer, 0]), axis=1),
            "up": jnp.concatenate(grid.gather_tp(uw[layer, 0]), axis=1),
            "down": jnp.concatenate(grid.gather_tp(dw[layer, 0]), axis=0),
        })

    last_grad = grid.gather_ep(tp_block(output_grad, 0, tp).astype(BF))

    stream = tp_block(tokens, 0, tp).astype(F32)
    saved = []
    for layer in range(layers):
        w = weights[layer]
        unit_one, inverse_one, normed_one = rms(stream, a_gain[layer])
        x = tp_join(grid.gather_tp(normed_one))
        part, kept_attention = attend(x, w, tables)
        residual = stream + grid.scatter_tp([tp_block(part, i, tp) for i in range(tp)])
        unit_two, inverse_two, normed_two = rms(residual, m_gain[layer])
        rows = jnp.concatenate(grid.gather_ep(normed_two), axis=0)
        out, kept_expert = expert(rows, every[layer], w)
        mixture = grid.scatter_ep(split(out, slots))
        stream = residual + mixture
        saved.append((x, unit_one, inverse_one, kept_attention, unit_two, inverse_two, normed_two, rows, kept_expert, mixture))
    block_output = tp_join(grid.gather_tp(stream.astype(BF)))

    stream_grad = tp_block(output_grad, 0, tp)
    shared, expert_grads = [None] * layers, [None] * layers
    for layer in reversed(range(layers)):
        w = weights[layer]
        (x, unit_one, inverse_one, kept_attention, unit_two, inverse_two, normed_two, rows, kept_expert, mixture) = saved[layer]
        arrived = last_grad if layer == layers - 1 else grid.gather_ep(stream_grad.astype(BF))
        sg = jnp.concatenate(arrived, axis=0)
        back, (d_gate, d_up, d_down, d_router) = expert_back(rows, sg, w, kept_expert)
        expert_grads[layer] = (
            grid.scatter_tp(jnp.split(d_gate, tp, axis=1)),
            grid.scatter_tp(jnp.split(d_up, tp, axis=1)),
            grid.scatter_tp(jnp.split(d_down, tp, axis=0)),
        )
        normed_grad = grid.scatter_ep(split(back, slots))
        weighted = jnp.sum(stream_grad * mixture, axis=-1, keepdims=True)
        shared_part = (-gates(normed_two, w["router"], chosen[layer]) * weighted).astype(BF)
        normed_grad = normed_grad + mm_nt(shared_part, w["router"])
        d_router = d_router + mm_tn(shared_part, normed_two)
        part, d_m_gain = rms_back(normed_grad, unit_two, inverse_two, m_gain[layer])
        residual_grad = stream_grad + part
        half = tp_join(grid.gather_tp(residual_grad.astype(BF)))
        grad_in, d_attention = attend_back(half, x, w, tables, kept_attention)
        normed_grad = grid.scatter_tp([tp_block(grad_in, i, tp) for i in range(tp)])
        part, d_a_gain = rms_back(normed_grad, unit_one, inverse_one, a_gain[layer])
        stream_grad = residual_grad + part
        small = jnp.concatenate([d_a_gain[None], d_m_gain[None], d_router], axis=0).astype(BF)
        shared[layer] = (
            [lax.psum(g.astype(BF), "ep").astype(F32) for g in d_attention],
            lax.psum(small, ("ep", "tp")).astype(F32),
        )
    input_grad = tp_join(grid.gather_tp(stream_grad.astype(BF))).astype(F32)
    big = [jnp.stack([shared[layer][0][i] for layer in range(layers)]) for i in range(4)]
    small = [shared[layer][1] for layer in range(layers)]
    e = [jnp.stack([expert_grads[layer][i] for layer in range(layers)])[:, None] for i in range(3)]
    return (
        block_output,
        input_grad,
        jnp.stack([s[0] for s in small]),
        *big,
        jnp.stack([s[1] for s in small]),
        jnp.stack([s[2:].T for s in small]),
        *e,
    )


def solution(mesh):
    grid = Grid(mesh)

    def step(*arguments):
        return on_device(grid, *arguments)

    return jax.shard_map(
        step,
        mesh=mesh,
        in_specs=(
            P("ep", None),
            P("ep"),
            P(None, "ep", None),
            P(),
            P(None, None, "tp"),
            P(None, None, "tp"),
            P(None, None, "tp"),
            P(None, "tp", None),
            P(),
            P(),
            P(None, "ep", None, "tp"),
            P(None, "ep", None, "tp"),
            P(None, "ep", "tp", None),
            P("ep", None),
        ),
        out_specs=(
            P("ep", None),
            P("ep", None),
            P(),
            P(None, None, "tp"),
            P(None, None, "tp"),
            P(None, None, "tp"),
            P(None, "tp", None),
            P(),
            P(),
            P(None, "ep", None, "tp"),
            P(None, "ep", None, "tp"),
            P(None, "ep", "tp", None),
        ),
        check_vma=False,
    )
```

```python
import jax
import jax.numpy as jnp
from jax import lax
from jax.sharding import PartitionSpec as P

HEAD = 64
EPS = 1e-06
THETA = 10000.0
SCALE = 0.125
NEGATIVE = -1e30
BF = jnp.bfloat16
F32 = jnp.float32


def mm(a, b):
    return jnp.dot(a, b, preferred_element_type=F32)


def mm_nt(a, b):
    return lax.dot_general(a, b, (((1,), (1,)), ((), ())), preferred_element_type=F32)


def mm_tn(a, b):
    return lax.dot_general(a, b, (((0,), (0,)), ((), ())), preferred_element_type=F32)


class Grid:
    def __init__(self, mesh):
        self.ep, self.tp = mesh.shape["ep"], mesh.shape["tp"]
        self.nc = 2 if self.ep % 2 == 0 else 1
        rest = self.ep // self.nc
        self.nz = 4 if rest % 4 == 0 else 1
        self.nx = rest // self.nz

    def move(self, value, dz=0, dx=0, dc=0, dt=0):
        pairs = []
        for z in range(self.nz):
            for x in range(self.nx):
                for c in range(self.nc):
                    for t in range(self.tp):
                        there = self.at(z + dz, x + dx, c + dc) * self.tp + (t + dt) % self.tp
                        pairs.append((self.at(z, x, c) * self.tp + t, there))
        return lax.ppermute(value, ("ep", "tp"), pairs)

    def at(self, z, x, c):
        return ((z % self.nz) * self.nx + x % self.nx) * self.nc + c % self.nc

    def slots(self):
        return [
            (k, j, d) for k in range(self.nz) for j in range(self.nx) for d in range(self.nc)
        ]

    def slot_owner(self, slot):
        me = lax.axis_index("ep")
        z, x, c = me // (self.nx * self.nc), (me // self.nc) % self.nx, me % self.nc
        z, x, c = (z - slot[0]) % self.nz, (x - slot[1]) % self.nx, (c - slot[2]) % self.nc
        return (z * self.nx + x) * self.nc + c

    def gather_ep(self, own):
        found = {(0, 0, 0): own}
        for k in range(self.nz):
            if k:
                found[k, 0, 0] = self.move(found[k - 1, 0, 0], dz=1)
            for j in range(1, self.nx):
                found[k, j, 0] = self.move(found[k, j - 1, 0], dx=1)
            for j in range(self.nx):
                for d in range(1, self.nc):
                    found[k, j, d] = self.move(found[k, j, d - 1], dc=1)
        return [found[slot] for slot in self.slots()]

    def scatter_ep(self, parts):
        part = dict(zip(self.slots(), parts, strict=True))
        terms = []
        for k in [*range(self.nz // 2, self.nz), *reversed(range(self.nz // 2))]:
            line = []
            for j in range(self.nx):
                total = part[k, j, self.nc - 1]
                for d in reversed(range(self.nc - 1)):
                    arrived = self.move(total, dc=1)
                    total = (arrived.astype(F32) + part[k, j, d].astype(F32)).astype(BF)
                line.append(total)
            total = line[-1]
            for j in reversed(range(self.nx - 1)):
                arrived = self.move(total, dx=-1)
                total = (arrived.astype(F32) + line[j].astype(F32)).astype(BF)
            terms.append(self.move(total, dz=-k) if k else total)
        return sum(term.astype(F32) for term in terms)

    def all_reduce_ep(self, value):
        c = lax.axis_index("ep") % self.nc
        x = lax.axis_index("ep") // self.nc % self.nx
        z = lax.axis_index("ep") // (self.nc * self.nx)
        for n, i, axis in ((self.nc, c, "dc"), (self.nx, x, "dx"), (self.nz, z, "dz")):
            total = block(value, i, n)
            for d in range(1, n):
                total = total + self.move(block(value, i - d, n).astype(BF), **{axis: -d}).astype(F32)
            value = total
        value = value.astype(BF)
        for n, i, axis in ((self.nz, z, "dz"), (self.nx, x, "dx"), (self.nc, c, "dc")):
            found = [value]
            for d in range(1, n):
                found.append(self.move(found[-1], **{axis: 1}))
            value = join(found, i)
        return value

    def all_reduce_small(self, value):
        value = value.astype(BF)
        for n, axis in ((self.tp, "dt"), (self.nc, "dc"), (self.nx, "dx"), (self.nz, "dz")):
            bit = 1
            while bit < n:
                other = self.swap(value, axis, bit)
                value = (value.astype(F32) + other.astype(F32)).astype(BF)
                bit *= 2
        return value

    def swap(self, value, axis, bit):
        pairs = []
        for z in range(self.nz):
            for x in range(self.nx):
                for c in range(self.nc):
                    for t in range(self.tp):
                        there = {"dz": z, "dx": x, "dc": c, "dt": t}
                        there[axis] ^= bit
                        target = self.at(there["dz"], there["dx"], there["dc"]) * self.tp + there["dt"]
                        pairs.append((self.at(z, x, c) * self.tp + t, target))
        return lax.ppermute(value, ("ep", "tp"), pairs)

    def gather_tp(self, own):
        found = [own]
        for _ in range(1, self.tp):
            found.append(self.move(found[-1], dt=1))
        return found

    def scatter_tp(self, parts):
        total = parts[0]
        for i in range(1, self.tp):
            total = total + self.move(parts[i].astype(BF), dt=-i).astype(F32)
        return total


def block(whole, i, n, axis=0):
    rows = whole.shape[axis] // n
    return lax.dynamic_slice_in_dim(whole, (i % n) * rows, rows, axis)


def join(blocks, i):
    n, rows = len(blocks), blocks[0].shape[0]
    whole = jnp.zeros((n * rows,) + blocks[0].shape[1:], blocks[0].dtype)
    for d, piece in enumerate(blocks):
        whole = lax.dynamic_update_slice_in_dim(whole, piece, ((i - d) % n) * rows, 0)
    return whole


def tp_block(whole, i, tp, axis=0):
    return block(whole, lax.axis_index("tp") - i, tp, axis)


def tp_join(blocks):
    return join(blocks, lax.axis_index("tp"))


def rope_tables(sequence_row):
    index_row = jnp.arange(sequence_row.shape[0], dtype=jnp.int32)
    same = sequence_row[:, None] == sequence_row[None, :]
    position = jnp.sum((same & (index_row[None, :] < index_row[:, None])).astype(jnp.int32), axis=1)
    half = HEAD // 2
    frequency = THETA ** (-(jnp.arange(half, dtype=F32) * 2.0 / HEAD))
    angle = position.astype(F32)[:, None] * frequency[None, :]
    allowed = same & (index_row[None, :] <= index_row[:, None])
    return jnp.cos(angle)[:, None, :], jnp.sin(angle)[:, None, :], allowed


def rotate(values, cosine, sine):
    first, second = values[..., : HEAD // 2], values[..., HEAD // 2 :]
    return jnp.concatenate(
        [first * cosine - second * sine, second * cosine + first * sine], axis=-1
    )


def rms(stream, gain):
    inverse = lax.rsqrt(jnp.mean(stream * stream, axis=-1, keepdims=True) + EPS)
    unit = stream * inverse
    return unit, inverse, (unit * gain).astype(BF)


def rms_back(grad, unit, inverse, gain):
    scaled = grad * gain
    back = inverse * (scaled - unit * jnp.mean(scaled * unit, axis=-1, keepdims=True))
    return back, jnp.sum(grad * unit, axis=0)


def attend(x, w, tables):
    cosine, sine, allowed = tables
    rows = x.shape[0]
    heads, groups = w["q"].shape[1] // HEAD, w["k"].shape[1] // HEAD
    q = rotate(mm(x, w["q"]).reshape(rows, heads, HEAD), cosine, sine).astype(BF)
    q = q.reshape(rows, groups, heads // groups, HEAD)
    k = rotate(mm(x, w["k"]).reshape(rows, groups, HEAD), cosine, sine).astype(BF)
    v = mm(x, w["v"]).astype(BF).reshape(rows, groups, HEAD)
    score = jnp.einsum("qngd,knd->ngqk", q, k, preferred_element_type=F32) * SCALE
    score = jnp.where(allowed, score, NEGATIVE)
    raised = jnp.exp(score - jnp.max(score, axis=-1, keepdims=True))
    probs = raised / jnp.sum(raised, axis=-1, keepdims=True)
    mixed = jnp.einsum("ngqk,knd->qngd", probs.astype(BF), v, preferred_element_type=F32)
    mixed = mixed.astype(BF).reshape(rows, heads * HEAD)
    return mm(mixed, w["o"]), (q, k, v, probs, mixed)


def attend_back(half, x, w, tables, kept):
    cosine, sine, allowed = tables
    q, k, v, probs, mixed = kept
    rows = x.shape[0]
    grad_o = mm_tn(mixed, half)
    mixed_grad = mm_nt(half, w["o"]).astype(BF).reshape(q.shape)
    prob_grad = jnp.einsum("qngd,knd->ngqk", mixed_grad, v, preferred_element_type=F32)
    row_dot = jnp.sum(probs * prob_grad, axis=-1, keepdims=True)
    score_grad = (probs * (prob_grad - row_dot) * SCALE).astype(BF)
    dv = jnp.einsum("ngqk,qngd->knd", probs.astype(BF), mixed_grad, preferred_element_type=F32)
    dk = jnp.einsum("ngqk,qngd->knd", score_grad, q, preferred_element_type=F32)
    dq = jnp.einsum("ngqk,knd->qngd", score_grad, k, preferred_element_type=F32)
    dq = rotate(dq.reshape(rows, -1, HEAD), cosine, -sine).astype(BF).reshape(rows, -1)
    dk = rotate(dk, cosine, -sine).astype(BF).reshape(rows, -1)
    dv = dv.astype(BF).reshape(rows, -1)
    grad_in = mm_nt(dq, w["q"]) + mm_nt(dk, w["k"]) + mm_nt(dv, w["v"])
    return grad_in, (mm_tn(x, jnp.concatenate([dq, dk, dv], axis=1)), grad_o)


def gates(normed, router, chosen):
    logits = jnp.where(chosen, mm(normed, router), NEGATIVE)
    raised = jnp.where(chosen, jnp.exp(logits - jnp.max(logits, axis=-1, keepdims=True)), 0.0)
    return raised / jnp.sum(raised, axis=-1, keepdims=True)


def expert(x, chosen, w):
    gate_all = gates(x, w["router"], chosen)
    p = lax.dynamic_slice_in_dim(gate_all, lax.axis_index("ep"), 1, 1)
    a, u = mm(x, w["gate"]), mm(x, w["up"])
    h = jax.nn.silu(a) * u
    scaled = (p * h).astype(BF)
    return mm(scaled, w["down"]).astype(BF), (p, a, u, h, scaled)


def expert_back(x, sg, w, kept):
    p, a, u, h, scaled = kept
    raw = mm_nt(sg, w["down"])
    pg = p * jnp.sum(h * raw, axis=-1, keepdims=True)
    hidden_grad = p * raw
    s = jax.nn.sigmoid(a)
    da = (hidden_grad * u * s * (1.0 + a * (1.0 - s))).astype(BF)
    du = (hidden_grad * (a * s)).astype(BF)
    here = lax.dynamic_slice_in_dim(w["router"], lax.axis_index("ep"), 1, 1)
    back = mm_nt(da, w["gate"]) + mm_nt(du, w["up"]) + pg * here.astype(F32).reshape(1, -1)
    column = jnp.sum(x.astype(F32) * pg, axis=0)
    mine = jnp.arange(w["router"].shape[1]) == lax.axis_index("ep")
    grad_router = jnp.where(mine[:, None], column[None, :], 0.0)
    return back.astype(BF), (mm_tn(x, da), mm_tn(x, du), mm_tn(scaled, sg), grad_router)


def split(whole, count):
    rows = whole.shape[0] // count
    return [whole[i * rows : (i + 1) * rows] for i in range(count)]


def on_device(grid, tokens, sequence_number, routes, a_gain, qw, kw, vw, ow, m_gain, router, gw, uw, dw, output_grad):
    tp, ep = grid.tp, grid.ep
    layers, experts = qw.shape[0], router.shape[2]
    assert gw.shape[1] == 1 and experts == ep
    slots = len(grid.slots())
    tables = rope_tables(sequence_number)

    own_routes = tp_block(routes, 0, tp, 1)
    rows, topk = own_routes.shape[1:]
    lines = own_routes.transpose(0, 2, 1).reshape(layers * topk, rows).astype(BF)
    lines = jnp.pad(lines, ((0, 0), (0, output_grad.shape[1] - rows)))
    first = jnp.concatenate([tp_block(output_grad, 0, tp).astype(BF), lines], axis=0)
    first = grid.gather_ep(first)
    last_grad = [arrived[:rows] for arrived in first]

    def named(ids):
        return jnp.any(ids[..., None] == jnp.arange(experts, dtype=ids.dtype), axis=-2)

    every = jnp.stack([arrived[rows:, :rows] for arrived in first])
    every = every.reshape(slots, layers, topk, rows).transpose(1, 0, 3, 2)
    every = named(every.astype(jnp.int32)).reshape(layers, slots * rows, experts)
    chosen = named(own_routes)

    weights = []
    for layer in range(layers):
        weights.append({
            "q": qw[layer], "k": kw[layer], "v": vw[layer], "o": ow[layer],
            "router": router[layer],
            "gate": jnp.concatenate(grid.gather_tp(gw[layer, 0]), axis=1),
            "up": jnp.concatenate(grid.gather_tp(uw[layer, 0]), axis=1),
            "down": jnp.concatenate(grid.gather_tp(dw[layer, 0]), axis=0),
        })

    stream = tp_block(tokens, 0, tp).astype(F32)
    saved = []
    for layer in range(layers):
        w = weights[layer]
        unit_one, inverse_one, normed_one = rms(stream, a_gain[layer])
        if layer:
            x = tp_join(grid.gather_tp(normed_one))
        else:
            x = rms(tokens.astype(F32), a_gain[layer])[2]
        part, kept_attention = attend(x, w, tables)
        residual = stream + grid.scatter_tp([tp_block(part, i, tp) for i in range(tp)])
        unit_two, inverse_two, normed_two = rms(residual, m_gain[layer])
        rows = jnp.concatenate(grid.gather_ep(normed_two), axis=0)
        out, kept_expert = expert(rows, every[layer], w)
        mixture = grid.scatter_ep(split(out, slots))
        stream = residual + mixture
        saved.append((x, unit_one, inverse_one, kept_attention, unit_two, inverse_two, normed_two, rows, kept_expert, mixture))
    block_output = tp_join(grid.gather_tp(stream.astype(BF)))

    stream_grad = tp_block(output_grad, 0, tp)
    shared, expert_grads = [None] * layers, [None] * layers
    for layer in reversed(range(layers)):
        w = weights[layer]
        (x, unit_one, inverse_one, kept_attention, unit_two, inverse_two, normed_two, rows, kept_expert, mixture) = saved[layer]
        arrived = last_grad if layer == layers - 1 else grid.gather_ep(stream_grad.astype(BF))
        sg = jnp.concatenate(arrived, axis=0)
        back, (d_gate, d_up, d_down, d_router) = expert_back(rows, sg, w, kept_expert)
        expert_grads[layer] = (
            grid.scatter_tp(jnp.split(d_gate, tp, axis=1)),
            grid.scatter_tp(jnp.split(d_up, tp, axis=1)),
            grid.scatter_tp(jnp.split(d_down, tp, axis=0)),
        )
        normed_grad = grid.scatter_ep(split(back, slots))
        weighted = jnp.sum(stream_grad * mixture, axis=-1, keepdims=True)
        shared_part = (-gates(normed_two, w["router"], chosen[layer]) * weighted).astype(BF)
        normed_grad = normed_grad + mm_nt(shared_part, w["router"])
        d_router = d_router + mm_tn(shared_part, normed_two)
        part, d_m_gain = rms_back(normed_grad, unit_two, inverse_two, m_gain[layer])
        residual_grad = stream_grad + part
        half = tp_join(grid.gather_tp(residual_grad.astype(BF)))
        grad_in, d_attention = attend_back(half, x, w, tables, kept_attention)
        normed_grad = grid.scatter_tp([tp_block(grad_in, i, tp) for i in range(tp)])
        part, d_a_gain = rms_back(normed_grad, unit_one, inverse_one, a_gain[layer])
        stream_grad = residual_grad + part
        small = jnp.concatenate([d_a_gain[None], d_m_gain[None], d_router], axis=0)
        shared[layer] = ([grid.all_reduce_ep(g).astype(F32) for g in d_attention], small)
    input_grad = tp_join(grid.gather_tp(stream_grad.astype(BF))).astype(F32)
    small = grid.all_reduce_small(jnp.concatenate([s[1] for s in shared], axis=0)).astype(F32)
    small = jnp.split(small, layers, axis=0)
    qkv = jnp.stack([s[0][0] for s in shared])
    n_q, n_k = qw.shape[2], kw.shape[2]
    big = [qkv[..., :n_q], qkv[..., n_q : n_q + n_k], qkv[..., n_q + n_k :], jnp.stack([s[0][1] for s in shared])]
    e = [jnp.stack([expert_grads[layer][i] for layer in range(layers)])[:, None] for i in range(3)]
    return (
        block_output,
        input_grad,
        jnp.stack([s[0] for s in small]),
        *big,
        jnp.stack([s[1] for s in small]),
        jnp.stack([s[2:].T for s in small]),
        *e,
    )


def solution(mesh):
    grid = Grid(mesh)

    def step(*arguments):
        return on_device(grid, *arguments)

    return jax.shard_map(
        step,
        mesh=mesh,
        in_specs=(
            P("ep", None),
            P("ep"),
            P(None, "ep", None),
            P(),
            P(None, None, "tp"),
            P(None, None, "tp"),
            P(None, None, "tp"),
            P(None, "tp", None),
            P(),
            P(),
            P(None, "ep", None, "tp"),
            P(None, "ep", None, "tp"),
            P(None, "ep", "tp", None),
            P("ep", None),
        ),
        out_specs=(
            P("ep", None),
            P("ep", None),
            P(),
            P(None, None, "tp"),
            P(None, None, "tp"),
            P(None, None, "tp"),
            P(None, "tp", None),
            P(),
            P(),
            P(None, "ep", None, "tp"),
            P(None, "ep", None, "tp"),
            P(None, "ep", "tp", None),
        ),
        check_vma=False,
    )
```

```python
import functools
import jax
import jax.numpy as jnp
from jax import lax
from jax.experimental import pallas as pl
from jax.experimental.pallas import tpu as pltpu
from jax.sharding import PartitionSpec as P

HEAD = 64
EPS = 1e-06
THETA = 10000.0
NEGATIVE = -1e30
BF = jnp.bfloat16
F32 = jnp.float32
ANY = pl.BlockSpec(memory_space=pl.ANY)
SMEM = pl.BlockSpec(memory_space=pltpu.SMEM)
VMEM = pl.BlockSpec(memory_space=pltpu.VMEM)


def mm(a, b):
    return jnp.dot(a, b, preferred_element_type=F32)


def mm_nt(a, b):
    return lax.dot_general(a, b, (((1,), (1,)), ((), ())), preferred_element_type=F32)


def mm_tn(a, b):
    return lax.dot_general(a, b, (((0,), (0,)), ((), ())), preferred_element_type=F32)


def struct(shape, dtype):
    return jax.ShapeDtypeStruct(shape, dtype)


class Copies:
    def __init__(self, sems):
        self.sems, self.used = sems, 0

    def start(self, source, target):
        copy = pltpu.make_async_copy(source, target, self.sems.at[self.used])
        self.used += 1
        copy.start()
        return copy


def call(body, outs, scratch, copies, flops, moved, vmem=67043328, specs=None, name=None):
    return functools.partial(
        _call, body, outs, scratch, copies, flops, moved, vmem, specs, name
    )


def _call(body, outs, scratch, copies, flops, moved, vmem, specs, name, *arguments):
    return pl.pallas_call(
        body,
        out_shape=outs,
        in_specs=specs or [ANY] * len(arguments),
        out_specs=jax.tree.map(lambda _: ANY, outs),
        scratch_shapes=[*scratch, pltpu.SemaphoreType.DMA((copies,))],
        compiler_params=pltpu.CompilerParams(vmem_limit_bytes=vmem),
        cost_estimate=pl.CostEstimate(flops=flops, bytes_accessed=moved, transcendentals=0),
        name=name,
    )(*arguments)


def wide(column, width):
    return jnp.concatenate([column] * (width // 128), axis=1)


class Weights:
    def __init__(self, arrays, layer=None):
        self.arrays, self.layer = arrays, layer
        self.tp = arrays[0].shape[0] if layer is None else len(arrays[0])
        self.hidden = arrays[2][0].shape[-2] * self.tp

    def operands(self):
        return list(self.arrays) if self.layer is None else [v for group in self.arrays for v in group]

    def blocks(self, refs):
        if self.layer is None:
            return [[ref.at[i] for i in range(self.tp)] for ref in refs]
        return [
            [refs[n * self.tp].at[self.layer, 0]] + list(refs[n * self.tp + 1 : (n + 1) * self.tp]) for n in range(3)
        ]

    def place(self, rank, i):
        return lax.rem(rank + self.tp - i, self.tp) if self.layer is None else i

    def load(self, copies, refs, targets):
        started = []
        for source, target, axis in zip(self.blocks(refs), targets, (1, 1, 0), strict=True):
            group = []
            for i, ref in enumerate(source):
                place = pl.ds(i * ref.shape[axis], ref.shape[axis])
                group.append(copies.start(ref, target.at[:, place] if axis else target.at[place]))
            started.append(group)
        return started


class Rows:
    def __init__(self, whole=None, chunks=None):
        self.whole, self.chunks = whole, chunks

    def operands(self, k=None):
        if self.whole is not None:
            return [self.whole]
        chunks = self.chunks if k is None else [self.chunks[k]]
        return [v for chunk in chunks for line in chunk for v in line]

    @staticmethod
    def source(refs, table, n, first, at, size):
        if len(refs) == 1:
            return refs[0].at[(table[1 + first + n], *at)]
        return refs[n] if refs[n].shape[0] == size else refs[n].at[at]


def ids_in_order(pieces, rows):
    count, whole = 128 // rows, []
    for first in range(0, len(pieces), count):
        joined = pieces[first]
        lane = lax.broadcasted_iota(jnp.int32, joined.shape, 1)
        for n in range(1, count):
            joined = jnp.where(lane >= n * rows, pieces[first + n], joined)
        whole.append(joined)
    return jnp.concatenate(whole, axis=1)


def expert_forward(layer, k, topk, experts, table, shards, payload, router, weights):
    tp, blocks = weights.tp, len(shards.chunks[k])
    flat, lines = shards.operands(k), payload.operands(k)
    rows, model = flat[0].shape
    per = len(flat) // blocks
    size = rows * per
    total = size * blocks
    hidden = weights.hidden
    below, places = lines[0].shape[-2] - rows, table.shape[0] - 2

    def body(*refs):
        index_ref, refs = refs[0], refs[1:]
        x_refs, refs = refs[: len(flat)], refs[len(flat) :]
        line_refs, refs = refs[: len(lines)], refs[len(lines) :]
        router_ref, refs = refs[0], refs[1:]
        weight_refs, refs = refs[: len(weights.operands())], refs[len(weights.operands()) :]
        out_refs, (a_ref, b_ref, h_ref), refs = refs[:blocks], refs[blocks : blocks + 3], refs[blocks + 3 :]
        x_s, ids_s, router_s, wg, wu, wd, o_s, a_s, b_s, h_s, sems = refs
        copies = Copies(sems)
        arrived = [[] for _ in range(blocks)]
        for i, ref in enumerate(x_refs):
            arrived[i // per].append(copies.start(ref, x_s.at[pl.ds(i * rows, rows)]))
            if i == per - 1:
                small = [copies.start(router_ref.at[layer], router_s)]
                for n in range(len(flat)):
                    source = Rows.source(line_refs, index_ref, n, k * len(flat), (pl.ds(rows, below), pl.ds(0, 128)), 0)
                    small.append(copies.start(source, ids_s.at[n]))
                gates, ups, downs = weights.load(copies, weight_refs, (wg, wu, wd))
        leaving = []
        for b in range(blocks):
            here = pl.ds(b * size, size)
            for copy in arrived[b]:
                copy.wait()
            if b == 0:
                for copy in small:
                    copy.wait()
            x = x_s[here]
            logits = jnp.transpose(mm(x, router_s[...]))[:experts]
            expert_row = lax.broadcasted_iota(jnp.int32, (experts, size), 0).astype(F32)
            named = ids_in_order([ids_s[b * per + n].astype(F32)[layer * topk : (layer + 1) * topk] for n in range(per)], rows)
            chosen = expert_row == named[0:1]
            for i in range(1, named.shape[0]):
                chosen = chosen | (expert_row == named[i : i + 1])
            logits = jnp.where(chosen, logits, NEGATIVE)
            raised = jnp.where(chosen, jnp.exp(logits - jnp.max(logits, axis=0, keepdims=True)), 0.0)
            share = jnp.sum(jnp.where(expert_row == index_ref[places + 1].astype(F32), raised, 0.0), axis=0, keepdims=True)
            share = share / jnp.sum(raised, axis=0, keepdims=True)
            p = wide(jnp.transpose(jnp.broadcast_to(share, (128, size))), hidden)
            if b == 0:
                for copy in gates:
                    copy.wait()
            a = mm(x, wg[...])
            if b == 0:
                for copy in ups:
                    copy.wait()
            u = mm(x, wu[...])
            s = 1.0 / (1.0 + jnp.exp(-a))
            gated = p * (a * s)
            a_s[here] = (p * u * (s * (1.0 + a * (1.0 - s)))).astype(BF)
            b_s[here] = gated.astype(BF)
            h = (gated * u).astype(BF)
            h_s[here] = h
            if b == 0:
                for copy in downs:
                    copy.wait()
            o_s[here] = mm(h, wd[...]).astype(BF)
            leaving.append(copies.start(o_s.at[here], out_refs[b]))
            for source, target in ((a_s, a_ref), (b_s, b_ref), (h_s, h_ref)):
                leaving.append(copies.start(source.at[here], target.at[here]))
        for copy in leaving:
            copy.wait()

    specs = [SMEM] + [ANY] * (len(flat) + len(lines) + 1 + len(weights.operands()))
    outs = [struct((size, model), BF)] * blocks + [struct((total, hidden), BF)] * 3
    scratch = [
        pltpu.VMEM((total, model), BF), pltpu.VMEM((len(flat), below, 128), BF),
        pltpu.VMEM(router.shape[1:], BF), pltpu.VMEM((model, hidden), BF), pltpu.VMEM((model, hidden), BF),
        pltpu.VMEM((hidden, model), BF), pltpu.VMEM((total, model), BF),
        pltpu.VMEM((total, hidden), BF), pltpu.VMEM((total, hidden), BF), pltpu.VMEM((total, hidden), BF),
    ]
    flops = 6 * total * model * hidden
    got = call(body, outs, scratch, 2 * len(flat) + 1 + 3 * tp + 4 * blocks, flops, 8 << 20, specs=specs, name="expert_forward")(
        table, *flat, *lines, router, *weights.operands()
    )
    return got[:blocks], got[blocks:]


def expert_backward(k, blocks, rows, table, shards, factors, router_row, weights):
    tp, model = weights.tp, router_row.shape[1]
    total, hidden = factors[0].shape
    size, flat, count = total // blocks, shards.operands(k), total // rows
    per = count // blocks

    def body(*refs):
        index_ref, refs = refs[0], refs[1:]
        g_refs_in, refs = refs[: len(flat)], refs[len(flat) :]
        (a_ref, b_ref, h_ref), row_ref, refs = refs[:3], refs[3], refs[4:]
        weight_refs, refs = refs[: len(weights.operands())], refs[len(weights.operands()) :]
        out_refs, (da_ref, du_ref, pg_ref), refs = refs[:blocks], refs[blocks : blocks + 3], refs[blocks + 3 :]
        x_s, a_s, b_s, h_s, row_s, wg, wu, wd, o_s, da_s, du_s, pg_s, sems = refs
        copies = Copies(sems)
        arrived = [[] for _ in range(blocks)]
        for i in range(count):
            source = Rows.source(g_refs_in, index_ref, i, k * count, (pl.ds(0, rows),), rows)
            arrived[i // per].append(copies.start(source, x_s.at[pl.ds(i * rows, rows)]))
            if i == per - 1:
                kept = [copies.start(source, target) for source, target in ((a_ref, a_s), (b_ref, b_s), (h_ref, h_s), (row_ref, row_s))]
                gates, ups, downs = weights.load(copies, weight_refs, (wg, wu, wd))
        leaving = []
        for b in range(blocks):
            here = pl.ds(b * size, size)
            for copy in arrived[b]:
                copy.wait()
            if b == 0:
                for copy in downs:
                    copy.wait()
            raw = mm_nt(x_s[here], wd[...])
            if b == 0:
                for copy in kept:
                    copy.wait()
            pg = jnp.sum(raw * h_s[here].astype(F32), axis=1, keepdims=True)
            da = (raw * a_s[here].astype(F32)).astype(BF)
            du = (raw * b_s[here].astype(F32)).astype(BF)
            da_s[here] = da
            du_s[here] = du
            pg_s[here] = jnp.broadcast_to(pg, (size, 128)).astype(BF)
            if b == 0:
                for copy in gates + ups:
                    copy.wait()
            back = mm_nt(da, wg[...]) + mm_nt(du, wu[...]) + pg * row_s[0:1]
            o_s[here] = back.astype(BF)
            leaving.append(copies.start(o_s.at[here], out_refs[b]))
            for source, target in ((da_s, da_ref), (du_s, du_ref), (pg_s, pg_ref)):
                leaving.append(copies.start(source.at[here], target.at[here]))
        for copy in leaving:
            copy.wait()

    outs = [struct((size, model), BF)] * blocks + [struct((total, hidden), BF)] * 2 + [struct((total, 128), BF)]
    scratch = [
        pltpu.VMEM((total, model), BF), pltpu.VMEM((total, hidden), BF), pltpu.VMEM((total, hidden), BF), pltpu.VMEM((total, hidden), BF),
        pltpu.VMEM((8, model), F32), pltpu.VMEM((model, hidden), BF), pltpu.VMEM((model, hidden), BF), pltpu.VMEM((hidden, model), BF),
        pltpu.VMEM((total, model), BF), pltpu.VMEM((total, hidden), BF), pltpu.VMEM((total, hidden), BF), pltpu.VMEM((total, 128), BF),
    ]
    got = call(body, outs, scratch, count + 4 + 3 * tp + 4 * blocks, 6 * total * model * hidden, 9 << 20, specs=[SMEM] + [ANY] * (len(flat) + 4 + len(weights.operands())), name="expert_backward")(
        table, *flat, *factors, router_row, *weights.operands()
    )
    return got[:blocks], got[blocks:]


def expert_weights(weights, rows, table, x_shards, g_shards, da, du, pg, h):
    chunks, tp = len(da), weights.tp
    flat_x, flat_g = x_shards.operands(), g_shards.operands()
    model = flat_x[0].shape[1]
    total, hidden = da[0].shape
    part, per = hidden // tp, total // rows

    def body(*refs):
        index_ref, refs = refs[0], refs[1:]
        x_refs, refs = refs[: len(flat_x)], refs[len(flat_x) :]
        g_refs, refs = refs[: len(flat_g)], refs[len(flat_g) :]
        small, refs = refs[: 4 * chunks], refs[4 * chunks :]
        outs, refs = refs[: 3 * tp + 1], refs[3 * tp + 1 :]
        x_s, g_s, da_s, du_s, pg_s, h_s, acc_g, acc_u, acc_d, acc_r, half_g, half_d, sems = refs
        copies = Copies(sems)
        arrived = []
        for c in range(chunks):
            group = []
            for i in range(per):
                place = pl.ds((c * per + i) * rows, rows)
                for source, target in ((x_refs, x_s), (g_refs, g_s)):
                    source = Rows.source(source, index_ref, c * per + i, 0, (pl.ds(0, rows),), rows)
                    group.append(copies.start(source, target.at[place]))
            for source, target in zip((small[c], small[chunks + c], small[2 * chunks + c], small[3 * chunks + c]), (da_s, du_s, pg_s, h_s), strict=True):
                group.append(copies.start(source, target.at[pl.ds(c * total, total)]))
            arrived.append(group)
        for c in range(chunks):
            here = pl.ds(c * total, total)
            for copy in arrived[c]:
                copy.wait()
            x, g = x_s[here], g_s[here]
            new = (mm_tn(x, da_s[here]), mm_tn(x, du_s[here]), mm_tn(h_s[here], g), mm_tn(pg_s[here], x))
            for acc, value in zip((acc_g, acc_u, acc_d, acc_r), new, strict=True):
                acc[...] = value if c == 0 else acc[...] + value
        leaving = []
        for i in range(tp):
            lanes = pl.ds(pl.multiple_of(weights.place(index_ref[0], i) * part, part), part)
            for n, acc in enumerate((acc_g, acc_u, acc_d)):
                source = acc.at[:, lanes] if n < 2 else acc.at[lanes]
                if i:
                    target = half_d.at[i - 1] if n == 2 else half_g.at[n, i - 1]
                    target[...] = source[...].astype(BF)
                    source = target
                leaving.append(copies.start(source, outs[n * tp + i]))
        leaving.append(copies.start(acc_r.at[pl.ds(0, 8)], outs[3 * tp]))
        for copy in leaving:
            copy.wait()

    kinds = [F32] + [BF] * (tp - 1)
    outs = [struct((model, part), kind) for _ in range(2) for kind in kinds] + [struct((part, model), kind) for kind in kinds]
    outs.append(struct((8, model), F32))
    length = chunks * total
    scratch = [
        pltpu.VMEM((length, model), BF), pltpu.VMEM((length, model), BF), pltpu.VMEM((length, hidden), BF), pltpu.VMEM((length, hidden), BF),
        pltpu.VMEM((length, 128), BF), pltpu.VMEM((length, hidden), BF),
        pltpu.VMEM((model, hidden), F32), pltpu.VMEM((model, hidden), F32), pltpu.VMEM((hidden, model), F32), pltpu.VMEM((128, model), F32),
        pltpu.VMEM((2, tp - 1, model, part), BF), pltpu.VMEM((tp - 1, part, model), BF),
    ]
    got = call(body, outs, scratch, chunks * (2 * per + 4) + 3 * tp + 1, 6 * length * model * hidden, 24 << 20, specs=[SMEM] + [ANY] * (len(flat_x) + len(flat_g) + 4 * chunks), name="expert_weights")(
        table, *flat_x, *flat_g, *da, *du, *pg, *h
    )
    return got[:tp], got[tp : 2 * tp], got[2 * tp : 3 * tp], got[3 * tp][0:1]


def turned(v):
    lane = lax.broadcasted_iota(jnp.int32, v.shape, 1)
    return jnp.where(lane % 64 < 32, pltpu.roll(v, 96, 1), pltpu.roll(v, 32, 1))


def twice(v, half):
    lane = lax.broadcasted_iota(jnp.int32, v.shape, 1)
    other = pltpu.roll(v, 64, 1)
    return jnp.where(lane < 64, v, other) if half == 0 else jnp.where(lane < 64, other, v)


def stacked(v):
    lane = lax.broadcasted_iota(jnp.int32, v.shape, 1)
    zero = jnp.zeros_like(v)
    return jnp.concatenate([jnp.where(lane < 64, v, zero), jnp.where(lane < 64, zero, v)], axis=0)


def unstacked(v):
    rows = v.shape[0] // 2
    top, bottom = v[:rows], v[rows:]
    lane = lax.broadcasted_iota(jnp.int32, top.shape, 1)
    return jnp.where(lane < 64, top, bottom)


def place_rows(copies, shards, target, rank, tp):
    if len(shards) == 1:
        return [copies.start(shards[0], target)]
    rows = shards[0].shape[0]
    return [
        copies.start(ref, target.at[pl.ds(pl.multiple_of(lax.rem(rank + tp - i, tp) * rows, rows), rows)])
        for i, ref in enumerate(shards)
    ]


def attention_forward(layer, tp, rank, shards, tables, bias, wq, wk, wv, wo):
    n_rows = bias.shape[0]
    model, n_q, n_k = wq.shape[1], wq.shape[2], wk.shape[2]
    width = n_q + 2 * n_k
    groups = n_q // 128
    rows = n_rows // tp

    def body(*refs):
        rank_ref, refs = refs[0], refs[1:]
        x_refs, refs = refs[: len(shards)], refs[len(shards) :]
        tab_ref, bias_ref, q_ref, k_ref, v_ref, o_ref, refs = *refs[:6], refs[6:]
        part_refs, (qkv_ref, p_ref, m_ref), refs = refs[:tp], refs[tp : tp + 3], refs[tp + 3 :]
        x_s, tab_s, bias_s, w_s, wo_s, qkv_s, p_s, m_s, own_s, send_s, sems = refs
        copies = Copies(sems)
        rank_here = rank_ref[0]
        arrived = place_rows(copies, x_refs, x_s, rank_here, tp)
        loads = [
            copies.start(q_ref.at[layer], w_s.at[:, pl.ds(0, n_q)]),
            copies.start(k_ref.at[layer], w_s.at[:, pl.ds(n_q, n_k)]),
            copies.start(v_ref.at[layer], w_s.at[:, pl.ds(n_q + n_k, n_k)]),
            copies.start(tab_ref, tab_s), copies.start(bias_ref, bias_s),
        ]
        last = copies.start(o_ref.at[layer], wo_s)
        for copy in arrived + loads:
            copy.wait()
        qkv = mm(x_s[...], w_s[...])
        cosine, sine = tab_s[0], tab_s[1]
        for lanes in range(0, n_q + n_k, 128):
            v = qkv[:, lanes : lanes + 128]
            qkv_s[:, lanes : lanes + 128] = (v * cosine + turned(v) * sine).astype(BF)
        qkv_s[:, n_q + n_k :] = qkv[:, n_q + n_k :].astype(BF)
        leaving = [copies.start(qkv_s, qkv_ref)]
        mask = bias_s[...]
        mask = jnp.concatenate([mask, mask], axis=0)
        for g in range(groups):
            k_at, v_at = n_q + g // 2 * 128, n_q + n_k + g // 2 * 128
            q = stacked(qkv_s[:, g * 128 : (g + 1) * 128])
            k = twice(qkv_s[:, k_at : k_at + 128], g % 2)
            v = twice(qkv_s[:, v_at : v_at + 128], g % 2)
            score = mm_nt(q, k) * 0.125 + mask
            raised = jnp.exp(score - jnp.max(score, axis=1, keepdims=True))
            p = (raised / jnp.sum(raised, axis=1, keepdims=True)).astype(BF)
            p_s[g] = p
            leaving.append(copies.start(p_s.at[g], p_ref.at[g]))
            m_s[:, g * 128 : (g + 1) * 128] = unstacked(mm(p, v)).astype(BF)
        leaving.append(copies.start(m_s, m_ref))
        last.wait()
        for i in reversed(range(tp)):
            here = pl.ds(pl.multiple_of(lax.rem(rank_here + tp - i, tp) * rows, rows), rows)
            part = mm(m_s[here], wo_s[...])
            if i:
                send_s[i - 1] = part.astype(BF)
                leaving.append(copies.start(send_s.at[i - 1], part_refs[i]))
            else:
                own_s[...] = part
                leaving.append(copies.start(own_s, part_refs[0]))
        for copy in leaving:
            copy.wait()

    outs = [struct((rows, model), F32)] + [struct((rows, model), BF)] * (tp - 1)
    outs += [struct((n_rows, width), BF), struct((groups, 2 * n_rows, n_rows), BF), struct((n_rows, n_q), BF)]
    scratch = [
        pltpu.VMEM((n_rows, model), BF), pltpu.VMEM(tables.shape, F32), pltpu.VMEM(bias.shape, F32), pltpu.VMEM((model, width), BF),
        pltpu.VMEM((n_q, model), BF), pltpu.VMEM((n_rows, width), BF), pltpu.VMEM((groups, 2 * n_rows, n_rows), BF),
        pltpu.VMEM((n_rows, n_q), BF), pltpu.VMEM((rows, model), F32), pltpu.VMEM((max(1, tp - 1), rows, model), BF),
    ]
    specs = [SMEM] + [ANY] * (len(shards) + 6)
    got = call(body, outs, scratch, len(shards) + 6 + groups + 2 + tp, 2 * n_rows * model * (width + n_q), 6 << 20, specs=specs, name="attention_forward")(
        rank, *shards, tables, bias, wq, wk, wv, wo
    )
    return got[:tp], got[tp:]


def attention_backward(layer, tp, rank, halves, tables, qkv, probs, wq, wk, wv, wo):
    n_rows, width = qkv.shape
    model, n_q, n_k = wq.shape[1], wq.shape[2], wk.shape[2]
    groups = n_q // 128
    rows = n_rows // tp

    def body(*refs):
        rank_ref, refs = refs[0], refs[1:]
        h_refs, refs = refs[:tp], refs[tp:]
        tab_ref, qkv_ref, p_ref, q_ref, k_ref, v_ref, o_ref, refs = *refs[:7], refs[7:]
        part_refs, (d_ref, half_ref), refs = refs[:tp], refs[tp : tp + 2], refs[tp + 2 :]
        half_s, tab_s, qkv_s, p_s, w_s, wo_s, d_s, k_s, v_s, own_s, send_s, sems = refs
        copies = Copies(sems)
        rank_here = rank_ref[0]
        first = place_rows(copies, h_refs, half_s, rank_here, tp) + [copies.start(o_ref.at[layer], wo_s)]
        second = [copies.start(qkv_ref, qkv_s), copies.start(p_ref, p_s), copies.start(tab_ref, tab_s)]
        third = [
            copies.start(q_ref.at[layer], w_s.at[:, pl.ds(0, n_q)]),
            copies.start(k_ref.at[layer], w_s.at[:, pl.ds(n_q, n_k)]),
            copies.start(v_ref.at[layer], w_s.at[:, pl.ds(n_q + n_k, n_k)]),
        ]
        for copy in first:
            copy.wait()
        leaving = [copies.start(half_s, half_ref)]
        mixed_grad = mm_nt(half_s[...], wo_s[...]).astype(BF)
        for copy in second:
            copy.wait()
        cosine, sine = tab_s[0], tab_s[1]

        def back(v):
            return (v * cosine - turned(v) * sine).astype(BF)

        for g in range(groups):
            pair, odd = g // 2 * 128, g % 2
            lanes = slice(g * 128, (g + 1) * 128)
            m = stacked(mixed_grad[:, lanes])
            q = stacked(qkv_s[:, lanes])
            k = twice(qkv_s[:, n_q + pair : n_q + pair + 128], odd)
            v = twice(qkv_s[:, n_q + n_k + pair : n_q + n_k + pair + 128], odd)
            half_p = p_s[g]
            p = half_p.astype(F32)
            prob_grad = mm_nt(m, v)
            row_dot = jnp.sum(p * prob_grad, axis=1, keepdims=True)
            score_grad = (p * (prob_grad - row_dot) * 0.125).astype(BF)
            d_s[:, lanes] = back(unstacked(mm(score_grad, k)))
            dk, dv = mm_tn(score_grad, q), mm_tn(half_p, m)
            dk, dv = dk + pltpu.roll(dk, 64, 1), dv + pltpu.roll(dv, 64, 1)
            if odd:
                lane = lax.broadcasted_iota(jnp.int32, dk.shape, 1)
                dk, dv = jnp.where(lane < 64, k_s[...], dk), jnp.where(lane < 64, v_s[...], dv)
            k_s[...] = dk
            v_s[...] = dv
            if odd or g == groups - 1:
                d_s[:, n_q + pair : n_q + pair + 128] = back(dk)
                d_s[:, n_q + n_k + pair : n_q + n_k + pair + 128] = dv.astype(BF)
        leaving.append(copies.start(d_s, d_ref))
        for copy in third:
            copy.wait()
        for i in reversed(range(tp)):
            here = pl.ds(pl.multiple_of(lax.rem(rank_here + tp - i, tp) * rows, rows), rows)
            part = mm_nt(d_s[here], w_s[...])
            if i:
                send_s[i - 1] = part.astype(BF)
                leaving.append(copies.start(send_s.at[i - 1], part_refs[i]))
            else:
                own_s[...] = part
                leaving.append(copies.start(own_s, part_refs[0]))
        for copy in leaving:
            copy.wait()

    outs = [struct((rows, model), F32)] + [struct((rows, model), BF)] * (tp - 1)
    outs += [struct((n_rows, width), BF), struct((n_rows, model), BF)]
    scratch = [
        pltpu.VMEM((n_rows, model), BF), pltpu.VMEM(tables.shape, F32), pltpu.VMEM((n_rows, width), BF), pltpu.VMEM(probs.shape, BF),
        pltpu.VMEM((model, width), BF), pltpu.VMEM((n_q, model), BF), pltpu.VMEM((n_rows, width), BF),
        pltpu.VMEM((n_rows, 128), F32), pltpu.VMEM((n_rows, 128), F32),
        pltpu.VMEM((rows, model), F32), pltpu.VMEM((max(1, tp - 1), rows, model), BF),
    ]
    specs = [SMEM] + [ANY] * (tp + 7)
    got = call(body, outs, scratch, tp + 1 + 3 + 3 + 2 + tp, 2 * n_rows * model * (width + n_q), 6 << 20, specs=specs, name="attention_backward")(
        rank, *halves, tables, qkv, probs, wq, wk, wv, wo
    )
    return got[:tp], got[tp], got[tp + 1]


def attention_weights(tp, cores, rank_core, shards, mixed, half, d_qkv, kind=F32):
    n_rows, width = d_qkv.shape
    model, n_q = half.shape[1], mixed.shape[1]
    part_m, part_q = model // cores, n_q // cores

    def body(*refs):
        rank_ref, refs = refs[0], refs[1:]
        x_refs, (m_ref, half_ref, d_ref), refs = refs[: len(shards)], refs[len(shards) : len(shards) + 3], refs[len(shards) + 3 :]
        o_refs, w_refs, refs = refs[:cores], refs[cores : 2 * cores], refs[2 * cores :]
        x_s, m_s, half_s, d_s, o_own, o_send, w_own, w_send, sems = refs
        copies = Copies(sems)
        rank_here, core = rank_ref[0], rank_ref[1]
        first = [copies.start(m_ref, m_s), copies.start(half_ref, half_s)]
        second = place_rows(copies, x_refs, x_s, rank_here, tp) + [copies.start(d_ref, d_s)]
        leaving = []
        for left, right, part, own, send, targets, waits in (
            (m_s, half_s, part_q, o_own, o_send, o_refs, first),
            (x_s, d_s, part_m, w_own, w_send, w_refs, second),
        ):
            for copy in waits:
                copy.wait()
            for i in reversed(range(cores)):
                place = pl.ds(pl.multiple_of(lax.rem(core + cores - i, cores) * part, part), part)
                value = mm_tn(left[:, place], right[...])
                if i:
                    send[i - 1] = value.astype(BF)
                    leaving.append(copies.start(send.at[i - 1], targets[i]))
                else:
                    own[...] = value.astype(kind)
                    leaving.append(copies.start(own, targets[0]))
        for copy in leaving:
            copy.wait()

    outs = [struct((part_q, model), kind)] + [struct((part_q, model), BF)] * (cores - 1)
    outs += [struct((part_m, width), kind)] + [struct((part_m, width), BF)] * (cores - 1)
    more = max(1, cores - 1)
    scratch = [
        pltpu.VMEM((n_rows, model), BF), pltpu.VMEM((n_rows, n_q), BF), pltpu.VMEM((n_rows, model), BF), pltpu.VMEM((n_rows, width), BF),
        pltpu.VMEM((part_q, model), kind), pltpu.VMEM((more, part_q, model), BF), pltpu.VMEM((part_m, width), kind), pltpu.VMEM((more, part_m, width), BF),
    ]
    specs = [SMEM] + [ANY] * (len(shards) + 3)
    got = call(body, outs, scratch, len(shards) + 3 + 2 * cores, 2 * n_rows * model * (width + n_q), 6 << 20, specs=specs, name="attention_weights")(
        rank_core, *shards, mixed, half, d_qkv
    )
    return got[:cores], got[cores:]


def small_call(body, name, outs, *arguments):
    moved = sum(v.size * v.dtype.itemsize for v in arguments)
    return pl.pallas_call(
        body,
        out_shape=outs,
        in_specs=[VMEM] * len(arguments),
        out_specs=jax.tree.map(lambda _: VMEM, outs),
        compiler_params=pltpu.CompilerParams(vmem_limit_bytes=6 << 20),
        cost_estimate=pl.CostEstimate(flops=moved, bytes_accessed=2 * moved, transcendentals=0),
        name=name,
    )(*arguments)


def unit_of(stream):
    inverse = lax.rsqrt(jnp.mean(stream * stream, axis=-1, keepdims=True) + EPS)
    return stream * inverse, inverse


def norm_back(grad, stream, gain):
    unit, inverse = unit_of(stream)
    scaled = grad * gain
    back = inverse * (scaled - unit * jnp.mean(scaled * unit, axis=-1, keepdims=True))
    return back, jnp.sum(grad * unit, axis=0, keepdims=True)


def total_of(refs):
    total = refs[0][...].astype(F32)
    for ref in refs[1:]:
        total = total + ref[...].astype(F32)
    return total


def norm_first(stream, gain):
    def body(s_ref, g_ref, x_ref):
        x_ref[...] = (unit_of(s_ref[...].astype(F32))[0] * g_ref[...]).astype(BF)

    return small_call(body, "norm_first", struct(stream.shape, BF), stream, gain)


def add(one, other):
    return (one.astype(F32) + other.astype(F32)).astype(BF)


def after(value, earlier):
    return value if earlier is None else lax.optimization_barrier((value, earlier))[0]


def after_attention(stream, parts, gain):
    def body(s_ref, g_ref, *refs):
        parts, (r_ref, n_ref) = refs[:-2], refs[-2:]
        residual = s_ref[...].astype(F32) + total_of(parts)
        r_ref[...] = residual
        n_ref[...] = (unit_of(residual)[0] * g_ref[...]).astype(BF)

    outs = [struct(stream.shape, F32), struct(stream.shape, BF)]
    return small_call(body, "after_attention", outs, stream, gain, *parts)


def after_experts(residual, terms, gain):
    def body(r_ref, *refs):
        if gain is not None:
            g_ref, refs = refs[0], refs[1:]
        terms, (m_ref, s_ref, n_ref) = refs[:-3], refs[-3:]
        mixture = total_of(terms)
        m_ref[...] = mixture
        stream = r_ref[...] + mixture
        s_ref[...] = stream
        n_ref[...] = (stream if gain is None else unit_of(stream)[0] * g_ref[...]).astype(BF)

    outs = [struct(residual.shape, F32), struct(residual.shape, F32), struct(residual.shape, BF)]
    extra = [] if gain is None else [gain]
    return small_call(body, "after_experts", outs, residual, *extra, *terms)


def experts_back(terms, stream_grad, mixture, residual, normed, gain, router, bias):
    def body(g_ref, m_ref, r_ref, n_ref, gain_ref, w_ref, b_ref, *refs):
        terms, (out_ref, half_ref, dg_ref, dr_ref) = refs[:-4], refs[-4:]
        grad = total_of(terms)
        outer = g_ref[...]
        weighted = jnp.sum(outer * m_ref[...], axis=1, keepdims=True)
        logits = mm(n_ref[...], w_ref[...]) + b_ref[...]
        raised = jnp.exp(logits - jnp.max(logits, axis=1, keepdims=True))
        p = raised / jnp.sum(raised, axis=1, keepdims=True)
        share = (-p * weighted).astype(BF)
        grad = grad + mm_nt(share, w_ref[...])
        dr_ref[...] = mm_tn(share, n_ref[...])
        back, dg = norm_back(grad, r_ref[...], gain_ref[...])
        dg_ref[...] = jnp.broadcast_to(dg, dg_ref.shape)
        out = outer + back
        out_ref[...] = out
        half_ref[...] = out.astype(BF)

    rows, model = residual.shape
    outs = [struct((rows, model), F32), struct((rows, model), BF), struct((8, model), F32), struct((128, model), F32)]
    return small_call(body, "experts_back", outs, stream_grad, mixture, residual, normed, gain, router, bias, *terms)


def attention_back_end(residual_grad, parts, stream, gain):
    def body(r_ref, s_ref, gain_ref, *refs):
        parts, (out_ref, half_ref, dg_ref) = refs[:-3], refs[-3:]
        back, dg = norm_back(total_of(parts), s_ref[...].astype(F32), gain_ref[...])
        dg_ref[...] = jnp.broadcast_to(dg, dg_ref.shape)
        out = r_ref[...] + back
        out_ref[...] = out
        half_ref[...] = out.astype(BF)

    rows, model = stream.shape
    outs = [struct((rows, model), F32), struct((rows, model), BF), struct((8, model), F32)]
    return small_call(body, "attention_back_end", outs, residual_grad, stream, gain, *parts)


class Grid:
    def __init__(self, mesh):
        self.ep, self.tp = mesh.shape["ep"], mesh.shape["tp"]
        self.nc, self.nz = 2, 4
        self.nx = self.ep // (self.nc * self.nz)
        assert self.nc * self.nz * self.nx == self.ep

    def at(self, z, x, c):
        return ((z % self.nz) * self.nx + x % self.nx) * self.nc + c % self.nc

    def owner(self, place, k, d, j):
        z, x, c = place // (self.nx * self.nc), place // self.nc % self.nx, place % self.nc
        return self.at(z - k, x - j, c - d)

    def permute(self, value, target):
        pairs = []
        for z in range(self.nz):
            for x in range(self.nx):
                for c in range(self.nc):
                    for t in range(self.tp):
                        z_to, x_to, c_to, t_to = target(z, x, c, t)
                        there = self.at(z_to, x_to, c_to) * self.tp + t_to % self.tp
                        pairs.append((self.at(z, x, c) * self.tp + t, there))
        return lax.ppermute(value, ("ep", "tp"), pairs)

    def move(self, value, dz=0, dx=0, dc=0, dt=0):
        return self.permute(value, lambda z, x, c, t: (z + dz, x + dx, c + dc, t + dt))

    def swap(self, value, axis, bit):
        def target(*place):
            place = list(place)
            place["zxct".index(axis)] ^= bit
            return place

        return self.permute(value, target)

    def gather_ep(self, own):
        chunks = []
        for k in range(self.nz):
            if k:
                own = self.move(own, dz=1)
            line = [own]
            for _ in range(1, self.nx):
                line.append(self.move(line[-1], dx=1))
            lines = [line]
            for _ in range(1, self.nc):
                lines.append([self.move(value, dc=1) for value in lines[-1]])
            chunks.append(lines)
        return chunks

    def order(self):
        return [*range(self.nz // 2, self.nz), *reversed(range(self.nz // 2))]

    def scatter_ep(self, parts):
        lines, terms, earlier = [], [], None
        for k in self.order():
            kept, sent = parts[k]
            total = add(after(kept, earlier), self.move(sent, dc=1))
            rows = total.shape[0] // self.nx
            lines.append([total[j * rows : (j + 1) * rows] for j in range(self.nx)])
            earlier = lines[-1][-1]
        for k, line in zip(self.order(), lines, strict=True):
            total = line[-1]
            for j in reversed(range(self.nx - 1)):
                total = add(after(line[j], earlier), self.move(total, dx=-1))
                earlier = total
            terms.append(self.move(total, dz=-k) if k else total)
        return terms

    def all_reduce_ep(self, by_core):
        c = lax.axis_index("ep") % self.nc
        x = lax.axis_index("ep") // self.nc % self.nx
        z = lax.axis_index("ep") // (self.nc * self.nx)
        value = by_core[0]
        for d in range(1, self.nc):
            value = value + self.move(by_core[d], dc=-d).astype(F32)
        for n, i, axis in ((self.nx, x, "dx"), (self.nz, z, "dz")):
            total = block(value, i, n)
            for d in range(1, n):
                total = total + self.move(block(value, i - d, n).astype(BF), **{axis: -d}).astype(F32)
            value = total
        value = value.astype(BF)
        for n, i, axis in ((self.nz, z, "dz"), (self.nx, x, "dx"), (self.nc, c, "dc")):
            found = [value]
            for d in range(1, n):
                found.append(self.move(found[-1], **{axis: 1}))
            value = join(found, i)
        return value

    def all_reduce_small(self, value):
        value = value.astype(BF)
        for n, axis in ((self.tp, "t"), (self.nc, "c"), (self.nx, "x"), (self.nz, "z")):
            bit = 1
            while bit < n:
                other = self.swap(value, axis, bit)
                value = (value.astype(F32) + other.astype(F32)).astype(BF)
                bit *= 2
        return value

    def gather_tp(self, own):
        found = [own]
        for _ in range(1, self.tp):
            found.append(self.move(found[-1], dt=1))
        return found

    def scatter_tp(self, parts):
        return [parts[0]] + [self.move(parts[i], dt=-i) for i in range(1, self.tp)]


def block(whole, i, n, axis=0):
    rows = whole.shape[axis] // n
    return lax.dynamic_slice_in_dim(whole, (i % n) * rows, rows, axis)


def join(blocks, i):
    n, rows = len(blocks), blocks[0].shape[0]
    whole = jnp.zeros((n * rows,) + blocks[0].shape[1:], blocks[0].dtype)
    for d, piece in enumerate(blocks):
        whole = lax.dynamic_update_slice_in_dim(whole, piece, ((i - d) % n) * rows, 0)
    return whole


def tp_block(whole, tp, axis=0):
    return block(whole, lax.axis_index("tp"), tp, axis)


def attention_tables(sequence_row):
    index_row = jnp.arange(sequence_row.shape[0], dtype=jnp.int32)
    same = sequence_row[:, None] == sequence_row[None, :]
    position = jnp.sum((same & (index_row[None, :] < index_row[:, None])).astype(jnp.int32), axis=1)
    half = HEAD // 2
    frequency = THETA ** (-(jnp.arange(half, dtype=F32) * 2.0 / HEAD))
    angle = position.astype(F32)[:, None] * frequency[None, :]
    cosine, sine = jnp.cos(angle), jnp.sin(angle)
    tables = jnp.stack([jnp.concatenate([cosine] * 4, axis=1), jnp.concatenate([-sine, sine, -sine, sine], axis=1)])
    allowed = same & (index_row[None, :] <= index_row[:, None])
    return tables, jnp.where(allowed, 0.0, NEGATIVE).astype(F32)


def on_device(grid, tokens, sequence_number, routes, a_gain, qw, kw, vw, ow, m_gain, router, gw, uw, dw, output_grad):
    tp, ep = grid.tp, grid.ep
    layers, experts = qw.shape[0], router.shape[2]
    assert gw.shape[1] == 1 and experts == ep
    model = tokens.shape[1]
    here = lax.axis_index("ep")
    rank = jnp.stack([lax.axis_index("tp"), here % grid.nc]).astype(jnp.int32)
    owners = [grid.owner(here, k, d, j) for k in range(grid.nz) for d in range(grid.nc) for j in range(grid.nx)]
    table = jnp.stack([lax.axis_index("tp"), *owners, here]).astype(jnp.int32)
    tables, bias = attention_tables(sequence_number)
    a_gain, m_gain = a_gain[:, None, :], m_gain[:, None, :]
    lanes = jnp.pad(router, ((0, 0), (0, 0), (0, 128 - experts)))
    router_rows = lax.dynamic_index_in_dim(router, here, 2, keepdims=False).astype(F32)
    router_rows = jnp.broadcast_to(router_rows[:, None, :], (layers, 8, model))

    weights = [Weights([[v] + grid.gather_tp(v[0, 0])[1:] for v in (gw, uw, dw)], 0)]

    own_routes = tp_block(routes, tp, 1)
    rows, topk = own_routes.shape[1:]
    lines = own_routes.transpose(0, 2, 1).reshape(layers * topk, rows).astype(BF)
    assert 128 % rows == 0 and layers * topk % 16 == 0
    lines = jnp.concatenate([lines] * (128 // rows), axis=1)
    lines = jnp.pad(lines, ((0, 0), (0, model - 128)))
    outer_grad = tp_block(output_grad, tp)
    last_grad = Rows(whole=lax.all_gather(jnp.concatenate([outer_grad.astype(BF), lines], axis=0), "ep"))
    for layer in range(1, layers):
        blocks = after((gw[layer, 0], uw[layer, 0], dw[layer, 0]), last_grad.whole)
        weights.append(Weights([lax.all_gather(v, "tp") for v in blocks]))
    chosen = jnp.any(own_routes[..., None] == jnp.arange(128, dtype=jnp.int32), axis=2)
    own_bias = jnp.where(chosen, 0.0, NEGATIVE).astype(F32)

    stream = tp_block(tokens, tp)
    x = [norm_first(tokens, a_gain[0])]
    saved = []
    for layer in range(layers):
        parts, kept = attention_forward(layer, tp, rank, x, tables, bias, qw, kw, vw, ow)
        residual, normed = after_attention(stream, grid.scatter_tp(parts), m_gain[layer])
        chunks = Rows(chunks=grid.gather_ep(normed))
        outs, factors = [], []
        for k in range(grid.nz):
            out, factor = expert_forward(layer, k, topk, experts, table, chunks, last_grad, lanes, weights[layer])
            outs.append(out)
            factors.append(factor)
        last = layer == layers - 1
        terms = grid.scatter_ep(outs)
        mixture, following, half = after_experts(residual, terms, None if last else a_gain[layer + 1])
        saved.append((x, stream, kept, residual, normed, chunks, factors, mixture))
        stream, x = following, grid.gather_tp(half)
    block_output = join(x, lax.axis_index("tp"))

    stream_grad, arrived = outer_grad, last_grad
    shared, small, expert_grads = [None] * layers, [None] * layers, [None] * layers
    for layer in reversed(range(layers)):
        x, stream, (qkv, probs, mixed), residual, normed, chunks, factors, mixture = saved[layer]
        outs, kept = [], []
        for k in range(grid.nz):
            out, keep = expert_backward(k, grid.nc, rows, table, arrived, factors[k], router_rows[layer], weights[layer])
            outs.append(out)
            kept.append(keep)
        terms = grid.scatter_ep(outs)
        residual_grad, half, d_m_gain, d_router = experts_back(
            terms, stream_grad, mixture, residual, normed, m_gain[layer], lanes[layer], own_bias[layer]
        )
        *grads, column = expert_weights(
            weights[layer], rows, table, chunks, arrived, [v[0] for v in kept], [v[1] for v in kept], [v[2] for v in kept], [v[2] for v in factors]
        )
        expert_grads[layer] = [grid.scatter_tp(g) for g in grads]
        mine = (jnp.arange(experts) == here)[:, None]
        d_router = d_router[:experts] + jnp.where(mine, column, 0.0)
        halves = grid.gather_tp(half)
        parts, d_qkv, half = attention_backward(layer, tp, rank, halves, tables, qkv, probs, qw, kw, vw, ow)
        stream_grad, half_grad, d_a_gain = attention_back_end(
            residual_grad, grid.scatter_tp(parts), stream, a_gain[layer]
        )
        if layer:
            d_o, d_w = attention_weights(tp, 1, rank, x, mixed, half, d_qkv, BF)
            shared[layer] = lax.psum([d_w[0], d_o[0]], "ep")
        else:
            d_o, d_w = attention_weights(tp, grid.nc, rank, x, mixed, half, d_qkv)
            shared[layer] = [grid.all_reduce_ep(d_w), grid.all_reduce_ep(d_o)]
        small[layer] = jnp.concatenate([d_a_gain[:1], d_m_gain[:1], d_router], axis=0)
        if layer:
            arrived = Rows(chunks=grid.gather_ep(half_grad))
    input_grad = join(grid.gather_tp(half_grad), lax.axis_index("tp")).astype(F32)
    small = grid.all_reduce_small(jnp.concatenate(small, axis=0)).astype(F32)
    small = jnp.split(small, layers, axis=0)
    qkv = jnp.stack([s[0] for s in shared]).astype(F32)
    n_q, n_k = qw.shape[2], kw.shape[2]

    def summed(i):
        terms = [[g.astype(F32) for g in expert_grads[layer][i]] for layer in range(layers)]
        return jnp.stack([sum(t[1:], t[0]) for t in terms])[:, None]

    return (
        block_output,
        input_grad,
        jnp.stack([s[0] for s in small]),
        qkv[..., :n_q],
        qkv[..., n_q : n_q + n_k],
        qkv[..., n_q + n_k :],
        jnp.stack([s[1] for s in shared]).astype(F32),
        jnp.stack([s[1] for s in small]),
        jnp.stack([s[2:].T for s in small]),
        summed(0),
        summed(1),
        summed(2),
    )


def solution(mesh):
    grid = Grid(mesh)

    def step(*arguments):
        return on_device(grid, *arguments)

    return jax.shard_map(
        step,
        mesh=mesh,
        in_specs=(
            P("ep", None),
            P("ep"),
            P(None, "ep", None),
            P(),
            P(None, None, "tp"),
            P(None, None, "tp"),
            P(None, None, "tp"),
            P(None, "tp", None),
            P(),
            P(),
            P(None, "ep", None, "tp"),
            P(None, "ep", None, "tp"),
            P(None, "ep", "tp", None),
            P("ep", None),
        ),
        out_specs=(
            P("ep", None),
            P("ep", None),
            P(),
            P(None, None, "tp"),
            P(None, None, "tp"),
            P(None, None, "tp"),
            P(None, "tp", None),
            P(),
            P(),
            P(None, "ep", None, "tp"),
            P(None, "ep", None, "tp"),
            P(None, "ep", "tp", None),
        ),
        check_vma=False,
    )
```
